32 devices in a mesh: pipe: 2 (over y), dp: 16 (over z, x, core).
Axes of the slice: x: 2, y: 2, z: 4, core: 2. Of those that a mesh axis runs over, the one named last changes fastest.
Arguments:
- tokens: bfloat16 [2, 8704, 768], P(None, 'dp'), may hold values from -6 to 6
- cotangent: bfloat16 [2, 8704, 768], P(None, 'dp'), may hold values from -6 to 6
- crop_lengths: int32 [2, 16, 6], P(None, 'dp'), may hold values from 0 to 197, as said below
- relative_index: int32 [197, 197], replicated, may hold values from 0 to 731
- first_gain: float32 [2, 768], P('pipe'), may hold values from 0.5 to 1.5
- first_shift: float32 [2, 768], P('pipe'), may hold values from -3 to 3
- attend_weight: bfloat16 [2, 768, 2304], P('pipe'), may hold values from -0.21875 to 0.21875
- query_bias: float32 [2, 768], P('pipe'), may hold values from -3 to 3
- value_bias: float32 [2, 768], P('pipe'), may hold values from -3 to 3
- relative_table: float32 [2, 732, 12], P('pipe'), may hold values from -4 to 4
- output_weight: bfloat16 [2, 768, 768], P('pipe'), may hold values from -1.75 to 1.75
- output_bias: float32 [2, 768], P('pipe'), may hold values from -3 to 3
- scale_one: float32 [2, 768], P('pipe'), may hold values from 0.5 to 1.5
- second_gain: float32 [2, 768], P('pipe'), may hold values from 0.5 to 1.5
- second_shift: float32 [2, 768], P('pipe'), may hold values from -3 to 3
- expand_weight: bfloat16 [2, 768, 3072], P('pipe'), may hold values from -0.21875 to 0.21875
- expand_bias: float32 [2, 3072], P('pipe'), may hold values from -3 to 3
- reduce_weight: bfloat16 [2, 3072, 768], P('pipe'), may hold values from -0.109375 to 0.109375
- reduce_bias: float32 [2, 768], P('pipe'), may hold values from -3 to 3
- scale_two: float32 [2, 768], P('pipe'), may hold values from 0.5 to 1.5
Outputs:
- outputs: bfloat16 [2, 2, 8704, 768], P('pipe', None, 'dp')
- input_grads: bfloat16 [2, 2, 8704, 768], P('pipe', None, 'dp')
- first_gain_gradient: float32 [2, 768], P('pipe')
- first_shift_gradient: float32 [2, 768], P('pipe')
- attend_weight_gradient: float32 [2, 768, 2304], P('pipe')
- query_bias_gradient: float32 [2, 768], P('pipe')
- value_bias_gradient: float32 [2, 768], P('pipe')
- relative_table_gradient: float32 [2, 732, 12], P('pipe')
- output_weight_gradient: float32 [2, 768, 768], P('pipe')
- output_bias_gradient: float32 [2, 768], P('pipe')
- scale_one_gradient: float32 [2, 768], P('pipe')
- second_gain_gradient: float32 [2, 768], P('pipe')
- second_shift_gradient: float32 [2, 768], P('pipe')
- expand_weight_gradient: float32 [2, 768, 3072], P('pipe')
- expand_bias_gradient: float32 [2, 3072], P('pipe')
- reduce_weight_gradient: float32 [2, 3072, 768], P('pipe')
- reduce_bias_gradient: float32 [2, 768], P('pipe')
- scale_two_gradient: float32 [2, 768], P('pipe')
The draws below stay inside these ranges and needn't reach their ends.
Inputs may be any that keep to these rules, and one draw needn't show every extreme that they name: `crop_lengths`: each image has two crops of 197 patches, then some local crops of 36 patches, then zeros, at most 4 local crops; in every micro-batch some image has 4 local crops.
All inputs are finite; a program needn't handle non-finite values.
Results may differ from the reference program's by a relative error of at most 0.015.
Values may be sent and summed in bfloat16 or wider, within the bound.
No kernel may reach another device: no remote copies, remote signals or barrier semaphores. Data moves between devices by JAX's collectives and lax.ppermute only.
A program may use at most 320 MiB of HBM per device.

```python
import jax
import jax.numpy as jnp
from jax import lax

D = 768
HEADS = 12
HEAD_DIM = 64
FF = 3072
GLOB = 197
LOC = 36
KMAX = 4
NREL = 732
MICRO = 2
NCROP = 6
SLOT = 544
IMAGES = 16
TOKENS = 8704


def draw_crop_lengths(key, part):
    first_draw = jax.random.randint(jax.random.fold_in(key, 11), (MICRO, IMAGES), 0, KMAX + 1, dtype=jnp.int32)
    second_draw = jax.random.randint(jax.random.fold_in(key, 12), (MICRO, IMAGES), 0, KMAX + 1, dtype=jnp.int32)
    chosen = jax.random.randint(jax.random.fold_in(key, 13), (MICRO,), 0, IMAGES, dtype=jnp.int32)
    counts = jnp.minimum(first_draw, second_draw)
    picked = jnp.arange(IMAGES, dtype=jnp.int32)[None, :] == chosen[:, None]
    counts = jnp.where(picked, KMAX, counts)
    column = jnp.arange(NCROP, dtype=jnp.int32)[None, None, :]
    local_part = jnp.where(column - 2 < counts[:, :, None], LOC, 0)
    return jnp.where(column < 2, GLOB, local_part).astype(jnp.int32)


def place_ends(drawn, own_key, low, largest):
    shape = drawn.shape
    spot = [jax.random.randint(jax.random.fold_in(own_key, axis), (), 0, shape[axis]) for axis in range(len(shape))]
    drawn = drawn.at[tuple(spot)].set(low)
    longest = shape.index(max(shape))
    spot[longest] = (spot[longest] + 1) % shape[longest]
    return drawn.at[tuple(spot)].set(largest)


def strengthened(values, own_key, source, target, parts, factor):
    def block_of(dim):
        return (jnp.arange(values.shape[dim]) // (values.shape[dim] // parts)).reshape((-1,) + (1,) * (values.ndim - 1 - dim))

    one_side = jax.random.permutation(own_key, parts)[block_of(target)]
    other_side = (block_of(target) + parts // 2) % parts
    return jnp.where((block_of(source) == one_side) | (block_of(source) == other_side), factor * values, values)


def block_scale(key, dims, cuts, low, top_value):
    def one(dim, blocks):
        steps = jax.random.uniform(jax.random.fold_in(jax.random.fold_in(key, 6), dim), (blocks,), jnp.float32, low / len(cuts), top_value / len(cuts))
        return jnp.repeat(jnp.exp(steps), dims[dim] // blocks).reshape((-1,) + (1,) * (len(dims) - dim - 1))

    loudness = one(*cuts[0])
    for cut in cuts[1:]:
        loudness = loudness * one(*cut)
    return loudness


def scatter_about(own_key, extent, scale, most, shards=(), kind=jnp.bfloat16):
    values = scale * jax.random.normal(own_key, extent, jnp.float32)
    if shards:
        values = values * block_scale(own_key, extent, shards, -0.22, 0.18)
    return jnp.clip(values, -most, most).astype(kind)


def bell_draw_with(rng, extent, spread, most, cuts, heavy, kind=jnp.bfloat16):
    entries = spread * jax.random.normal(rng, extent, jnp.float32)
    if cuts:
        entries = entries * block_scale(rng, extent, cuts, -0.22, 0.18)
    return jnp.clip(strengthened(entries, jax.random.fold_in(rng, 3), *heavy), -most, most).astype(kind)


def setup_inputs(seed: int = 0) -> dict:
    streams_of = jax.random.split(jax.random.key(seed), 21)
    tokens = scatter_about(streams_of[0], (MICRO, TOKENS, D), 1.0, 6.0, ((1, 16),))
    cotangent = bell_draw_with(streams_of[1], (MICRO, TOKENS, D), 1.0, 6.0, ((1, 16),), (1, 2, 16, 2.0))
    crop_lengths = draw_crop_lengths(jax.random.fold_in(streams_of[20], 71), 0)
    relative_index = place_ends(jax.random.randint(streams_of[3], (GLOB, GLOB), 0, NREL), jax.random.fold_in(streams_of[3], 1), 0, NREL - 1).astype(jnp.int32)
    first_gain = jnp.clip(1.0 + 0.1 * jax.random.normal(streams_of[4], (2, D), jnp.float32), 0.5, 1.5)
    first_shift = scatter_about(streams_of[5], (2, D), 0.5, 3.0, ((0, 2),), jnp.float32)
    attend_weight = scatter_about(streams_of[6], (2, D, 3 * D), D ** -0.5, 0.21875, ((0, 2),))
    query_bias = scatter_about(streams_of[7], (2, D), 0.5, 3.0, ((0, 2),), jnp.float32)
    value_bias = scatter_about(streams_of[8], (2, D), 0.5, 3.0, ((0, 2),), jnp.float32)
    relative_table = scatter_about(streams_of[9], (2, NREL, HEADS), 1.0, 4.0, ((0, 2),), jnp.float32)
    output_weight = scatter_about(streams_of[10], (2, D, D), (D // 64) ** -0.5, 1.75, ((0, 2),))
    output_bias = scatter_about(streams_of[11], (2, D), 0.5, 3.0, ((0, 2),), jnp.float32)
    scale_one = jnp.clip(0.5 + 1.0 * jax.random.uniform(streams_of[12], (2, D), jnp.float32) ** block_scale(streams_of[12], (2, D), ((0, 2),), -0.2, 0.2), 0.5, 1.5)
    second_gain = jnp.clip(1.0 + 0.1 * jax.random.normal(streams_of[13], (2, D), jnp.float32), 0.5, 1.5)
    second_shift = scatter_about(streams_of[14], (2, D), 0.5, 3.0, ((0, 2),), jnp.float32)
    expand_weight = scatter_about(streams_of[15], (2, D, FF), D ** -0.5, 0.21875, ((0, 2),))
    expand_bias = scatter_about(streams_of[16], (2, FF), 0.5, 3.0, ((0, 2),), jnp.float32)
    reduce_weight = scatter_about(streams_of[17], (2, FF, D), FF ** -0.5, 0.109375, ((0, 2),))
    reduce_bias = scatter_about(streams_of[18], (2, D), 0.5, 3.0, ((0, 2),), jnp.float32)
    scale_two = jnp.clip(0.5 + 1.0 * jax.random.uniform(streams_of[19], (2, D), jnp.float32) ** block_scale(streams_of[19], (2, D), ((0, 2),), -0.2, 0.2), 0.5, 1.5)
    return dict(tokens=tokens, cotangent=cotangent, crop_lengths=crop_lengths, relative_index=relative_index, first_gain=first_gain, first_shift=first_shift, attend_weight=attend_weight, query_bias=query_bias, value_bias=value_bias, relative_table=relative_table, output_weight=output_weight, output_bias=output_bias, scale_one=scale_one, second_gain=second_gain, second_shift=second_shift, expand_weight=expand_weight, expand_bias=expand_bias, reduce_weight=reduce_weight, reduce_bias=reduce_bias, scale_two=scale_two)


@jax.custom_vjp
def low(v):
    return lax.optimization_barrier(v.astype(jnp.bfloat16)).astype(jnp.float32)

@jax.custom_vjp
def low_back(v):
    return v

def low_keep(v):
    return (low(v), None)

def low_pass(kept, grad):
    return (grad,)

def back_keep(v):
    return (v, None)

def back_low(kept, grad):
    return (low(grad),)
low.defvjp(low_keep, low_pass)
low_back.defvjp(back_keep, back_low)
EPSILON = 1e-06
NEGATIVE = -1e+30

def layout(lengths, slot_rows, limit):
    crop_count = lengths.shape[0]
    crop_ends = jnp.cumsum(lengths, dtype=jnp.int32)
    starts = crop_ends - lengths
    places = jnp.arange(slot_rows, dtype=jnp.int32)
    segment = lax.optimization_barrier(jnp.sum((places[:, None] >= crop_ends[None, :]).astype(jnp.int32), axis=1, dtype=jnp.int32))
    begins = jnp.concatenate([starts, crop_ends[crop_count - 1:]])
    labels = jnp.arange(crop_count + 1, dtype=jnp.int32)
    start_at = lax.optimization_barrier(jnp.sum(jnp.where(segment[:, None] == labels[None, :], begins[None, :], 0), axis=1, dtype=jnp.int32))
    position = jnp.minimum(places - start_at, limit - 1)
    valid_rows = (segment < crop_count).astype(jnp.float32)
    return (segment, position, valid_rows)

def layer_norm(values, gain_vector, shift_vector):
    average = lax.optimization_barrier(jnp.mean(values, axis=-1, keepdims=True))
    centred = values - average
    variance = lax.optimization_barrier(jnp.mean(centred * centred, axis=-1, keepdims=True))
    return centred * lax.rsqrt(variance + EPSILON) * gain_vector + shift_vector

def matmul(earlier, later):
    return jnp.dot(earlier, later, precision=lax.Precision.HIGHEST, preferred_element_type=jnp.float32)

def layer_apply(params, values, lengths, relative_index):
    first_gain, first_shift, attend_weight, query_bias, value_bias, relative_table, output_weight, output_bias, scale_one, second_gain, second_shift, expand_weight, expand_bias, reduce_weight, reduce_bias, scale_two = params
    slot_rows = values.shape[0]
    segment, position, valid_rows = layout(lengths, slot_rows, GLOB)
    normed = low(layer_norm(values, first_gain, first_shift))
    offsets = jnp.concatenate([query_bias, jnp.zeros_like(query_bias), value_bias])
    factors = jnp.concatenate([jnp.full_like(query_bias, HEAD_DIM ** (-0.5)), jnp.ones_like(query_bias), jnp.ones_like(query_bias)])
    packed = low_back(low((matmul(normed, attend_weight) + offsets) * factors))
    queries = packed[:, :D].reshape(slot_rows, HEADS, HEAD_DIM)
    key_rows = packed[:, D:2 * D].reshape(slot_rows, HEADS, HEAD_DIM)
    value_rows = packed[:, 2 * D:].reshape(slot_rows, HEADS, HEAD_DIM)
    bias_grid = jnp.transpose(relative_table[relative_index], (2, 0, 1))
    scores = jnp.einsum('ihd,jhd->hij', queries, key_rows, precision=lax.Precision.HIGHEST)
    scores = scores + bias_grid[:, position[:, None], position[None, :]]
    allowed = segment[:, None] == segment[None, :]
    scores = low_back(jnp.where(allowed[None], scores, NEGATIVE))
    weights = low(jax.nn.softmax(scores, axis=-1))
    attended = jnp.einsum('hij,jhd->ihd', weights, value_rows, precision=lax.Precision.HIGHEST).reshape(slot_rows, D)
    attended = low_back(low(attended))
    branch = low_back(matmul(attended, output_weight) + output_bias)
    middle = values + scale_one * branch
    hidden_in = low(layer_norm(middle, second_gain, second_shift))
    hidden = low_back(matmul(hidden_in, expand_weight) + expand_bias)
    activated = low(jax.nn.gelu(hidden, approximate=False))
    mixed = low_back(matmul(activated, reduce_weight) + reduce_bias)
    return (middle + scale_two * mixed) * valid_rows[:, None]

def reference(tokens, cotangent, crop_lengths, relative_index, first_gain, first_shift, attend_weight, query_bias, value_bias, relative_table, output_weight, output_bias, scale_one, second_gain, second_shift, expand_weight, expand_bias, reduce_weight, reduce_bias, scale_two):
    stacked = tuple((member.astype(jnp.float32) for member in (first_gain, first_shift, attend_weight, query_bias, value_bias, relative_table, output_weight, output_bias, scale_one, second_gain, second_shift, expand_weight, expand_bias, reduce_weight, reduce_bias, scale_two)))
    first_layer = tuple((member[0] for member in stacked))
    second_layer = tuple((member[1] for member in stacked))
    image_total = MICRO * IMAGES
    inputs = tokens.astype(jnp.float32).reshape(image_total, SLOT, D)
    cotangents = cotangent.astype(jnp.float32).reshape(image_total, SLOT, D)
    lengths_all = crop_lengths.reshape(image_total, NCROP)

    def forward_pass(params, layer_in):

        def advance(unused_carry, member):
            return (unused_carry, layer_apply(params, member[0], member[1], relative_index).astype(jnp.bfloat16))
        unused_carry, results = lax.scan(advance, jnp.zeros((), jnp.float32), (layer_in, lengths_all))
        return results

    def backward_pass(params, layer_in, incoming):

        def advance(totals, member):
            layer_out, pullback = jax.vjp(lambda weights, entering: layer_apply(weights, entering, member[1], relative_index), params, member[0])
            gradients, entering_grad = pullback(member[2])
            totals = jax.tree.map(lambda earlier, later: earlier + later, totals, gradients)
            return (totals, (layer_out.astype(jnp.bfloat16), entering_grad.astype(jnp.bfloat16)))
        zero_grads = jax.tree.map(jnp.zeros_like, params)
        return lax.scan(advance, zero_grads, (layer_in, lengths_all, incoming))
    first_out = forward_pass(first_layer, inputs)
    second_grads, (second_out, second_back) = backward_pass(second_layer, first_out.astype(jnp.float32), cotangents)
    first_grads, (repeat_out, first_back) = backward_pass(first_layer, inputs, second_back.astype(jnp.float32))
    full_shape = (2, MICRO, IMAGES * SLOT, D)
    outputs = jnp.stack([first_out, second_out]).reshape(full_shape)
    input_grads = jnp.stack([first_back, second_back]).reshape(full_shape)
    joined = tuple((jnp.stack([earlier, later]) for earlier, later in zip(first_grads, second_grads)))
    return (outputs, input_grads, joined[0], joined[1], joined[2], joined[3], joined[4], joined[5], joined[6], joined[7], joined[8], joined[9], joined[10], joined[11], joined[12], joined[13], joined[14], joined[15])
```

```python
import functools
import math

import jax
import jax.numpy as jnp
from jax import lax
from jax.experimental import pallas as pl
from jax.experimental.pallas import tpu as pltpu
from jax.sharding import PartitionSpec as P

F32 = jnp.float32
BF16 = jnp.bfloat16
EPSILON = 1e-06
HEAD_DIM = 64
GLOB = 197
LOC = 36
GPAD = 208
LPAD = 48
HALF = GPAD + 2 * LPAD
PIECES = 4
NEGATIVE = -1e30
VMEM_LIMIT = 56 * 1024 * 1024


def dot_nn(a, b):
    return jnp.dot(a, b, preferred_element_type=F32)


def dot_nt(a, b):
    return lax.dot_general(a, b, (((1,), (1,)), ((), ())), preferred_element_type=F32)


def dot_tn(a, b):
    return lax.dot_general(a, b, (((0,), (0,)), ((), ())), preferred_element_type=F32)


def standardise(values):
    average = jnp.mean(values, axis=-1, keepdims=True)
    centred = values - average
    inverse = lax.rsqrt(jnp.mean(centred * centred, axis=-1, keepdims=True) + EPSILON)
    return centred * inverse, inverse


def norm_back(incoming, standard, inverse, gain):
    scaled = incoming * gain
    return inverse * (
        scaled
        - jnp.mean(scaled, axis=-1, keepdims=True)
        - standard * jnp.mean(scaled * standard, axis=-1, keepdims=True)
    )


def col_sum(values):
    return jnp.sum(values, axis=0, keepdims=True)


def params(n=1):
    return pltpu.CompilerParams(
        dimension_semantics=("arbitrary",) * n, vmem_limit_bytes=VMEM_LIMIT
    )


def row_valid(sc):
    row = lax.broadcasted_iota(jnp.int32, (HALF, 1), 0)
    local = jnp.where(row < GPAD + LPAD, GPAD + sc[6], GPAD + LPAD + sc[7])
    limit = jnp.where(row < GPAD, sc[5], local)
    return jnp.where(row < limit, 1.0, 0.0)


def cost(us):
    return pl.CostEstimate(flops=int(us * 1.1e9), bytes_accessed=int(us * 1e6), transcendentals=0)


def half_mask(shape, which):
    lane = lax.broadcasted_iota(jnp.int32, shape, 1)
    return (lane < HEAD_DIM) if which == 0 else (lane >= HEAD_DIM)


def attn_fwd_body(sc, tok, arr, g1, b1, wq, wk, wv, bq, bv, wo, grid, bo, s1, g2, b2, *rest):
    outs = rest[len(rest) - 2 - 9 : len(rest) - 2]
    xs, qs, ks, vs, pgs, pls, os_, atts, bs = outs
    a_s, acc = rest[-2:]
    step = pl.program_id(0)

    @pl.when(step == 0)
    def _():
        x = jnp.where(sc[2] == 0, tok[0], arr[...])
        xs[0] = x
        standard, _ = standardise(x.astype(F32))
        a_s[...] = (standard * g1[...] + b1[...]).astype(BF16)
        acc[...] = jnp.zeros_like(acc)

    a = a_s[...]
    q = ((dot_nn(a, wq[...]) + bq[...]) * HEAD_DIM ** (-0.5)).astype(BF16)
    k = dot_nn(a, wk[...]).astype(BF16)
    v = (dot_nn(a, wv[...]) + bv[...]).astype(BF16)
    qs[0] = q
    ks[0] = k
    vs[0] = v
    zero = jnp.zeros((HALF, 128), BF16)
    for pair in range(2):
        lanes = slice(pair * 128, pair * 128 + 128)
        qp, kp, vp = q[:, lanes], k[:, lanes], v[:, lanes]
        out_g = None
        out_l = [None, None]
        for hh in range(2):
            head = pair * 2 + hh
            mask = half_mask((HALF, 128), hh)
            km = jnp.where(mask, kp, zero)
            vm = jnp.where(mask, vp, zero)
            s = dot_nt(qp[:GPAD], km[:GPAD]) + grid[head]
            e = jnp.exp(s - jnp.max(s, axis=-1, keepdims=True))
            p = e * (1.0 / jnp.sum(e, axis=-1, keepdims=True))
            pgs[0, head] = p
            o = dot_nn(p.astype(BF16), vm[:GPAD])
            out_g = o if out_g is None else out_g + o
            column = lax.broadcasted_iota(jnp.int32, (LPAD, LPAD), 1)
            bias = jnp.where(column < LOC, grid[head, :LPAD, :LPAD], NEGATIVE)
            for j in range(2):
                rows = slice(GPAD + j * LPAD, GPAD + (j + 1) * LPAD)
                s = dot_nt(qp[rows], km[rows]) + bias
                e = jnp.exp(s - jnp.max(s, axis=-1, keepdims=True))
                p = e * (1.0 / jnp.sum(e, axis=-1, keepdims=True))
                pls[0, head, j] = p
                o = dot_nn(p.astype(BF16), vm[rows])
                out_l[j] = o if out_l[j] is None else out_l[j] + o
        os_[0, :GPAD, lanes] = out_g.astype(BF16)
        for j in range(2):
            os_[0, GPAD + j * LPAD : GPAD + (j + 1) * LPAD, lanes] = out_l[j].astype(BF16)
    acc[...] += dot_nn(os_[0], wo[...])

    @pl.when(step == pl.num_programs(0) - 1)
    def _():
        att = acc[...] + bo[...]
        atts[0] = att
        x1 = xs[0].astype(F32) + s1[...] * att
        standard, _ = standardise(x1)
        bs[0] = (standard * g2[...] + b2[...]).astype(BF16)


def attn_fwd(sc, tok, arr, vec, wa, wo, grid, bufs):
    d = wo.shape[0]
    heads = grid.shape[0]
    groups = d // 256
    per = heads // groups
    whole = pl.BlockSpec((1, d), lambda i, s: (0, 0))
    slot = lambda i, s: (s[0], 0, 0)
    chunk = lambda i, s: (s[0], 0, i)
    n = PIECES + 1
    shapes = [
        jax.ShapeDtypeStruct((n, HALF, d), BF16),
        jax.ShapeDtypeStruct((n, HALF, d), BF16),
        jax.ShapeDtypeStruct((n, HALF, d), BF16),
        jax.ShapeDtypeStruct((n, HALF, d), BF16),
        jax.ShapeDtypeStruct((n, heads, GPAD, GPAD), F32),
        jax.ShapeDtypeStruct((n, heads, 2, LPAD, LPAD), F32),
        jax.ShapeDtypeStruct((n, HALF, d), BF16),
        jax.ShapeDtypeStruct((n, HALF, d), F32),
        jax.ShapeDtypeStruct((n, HALF, d), BF16),
    ]
    out_specs = [
        pl.BlockSpec((1, HALF, d), slot),
        pl.BlockSpec((1, HALF, 256), chunk),
        pl.BlockSpec((1, HALF, 256), chunk),
        pl.BlockSpec((1, HALF, 256), chunk),
        pl.BlockSpec((1, per, GPAD, GPAD), lambda i, s: (s[0], i, 0, 0)),
        pl.BlockSpec((1, per, 2, LPAD, LPAD), lambda i, s: (s[0], i, 0, 0, 0)),
        pl.BlockSpec((1, HALF, 256), chunk),
        pl.BlockSpec((1, HALF, d), slot),
        pl.BlockSpec((1, HALF, d), slot),
    ]
    in_specs = [
        pl.BlockSpec((1, HALF, d), lambda i, s: (s[1], 0, 0)),
        pl.BlockSpec((HALF, d), lambda i, s: (0, 0)),
        whole,
        whole,
        pl.BlockSpec((d, 256), lambda i, s: (0, i)),
        pl.BlockSpec((d, 256), lambda i, s: (0, groups + i)),
        pl.BlockSpec((d, 256), lambda i, s: (0, 2 * groups + i)),
        pl.BlockSpec((1, 256), lambda i, s: (0, i)),
        pl.BlockSpec((1, 256), lambda i, s: (0, i)),
        pl.BlockSpec((256, d), lambda i, s: (i, 0)),
        pl.BlockSpec((per, GPAD, GPAD), lambda i, s: (i, 0, 0)),
        whole,
        whole,
        whole,
        whole,
    ]
    args = [tok, arr, vec["g1"], vec["b1"], wa, wa, wa, vec["bq"], vec["bv"], wo, grid,
            vec["bo"], vec["s1"], vec["g2"], vec["b2"]]
    alias = {}
    if bufs is not None:
        alias = {1 + len(args) + j: j for j in range(len(bufs))}
        args = args + list(bufs)
        in_specs = in_specs + [pl.BlockSpec(memory_space=pl.ANY)] * len(bufs)
    return pl.pallas_call(
        attn_fwd_body,
        out_shape=shapes,
        grid_spec=pltpu.PrefetchScalarGridSpec(
            num_scalar_prefetch=1,
            grid=(groups,),
            in_specs=in_specs,
            out_specs=out_specs,
            scratch_shapes=[pltpu.VMEM((HALF, d), BF16), pltpu.VMEM((HALF, d), F32)],
        ),
        compiler_params=params(),
        input_output_aliases=alias,
        name="attn_fwd",
        cost_estimate=cost(14),
    )(sc, *args)


def mlp_fwd_body(sc, x, att, b, w1, c1, w2, c2, s1, s2, *rest):
    gs, ts, ms, ys, sent = rest[-6:-1]
    acc = rest[-1]
    step = pl.program_id(0)

    @pl.when(step == 0)
    def _():
        acc[...] = jnp.zeros_like(acc)

    h = dot_nn(b[0], w1[...]) + c1[...]
    cdf = 0.5 * (1.0 + lax.erf(h * (1.0 / math.sqrt(2.0))))
    g = (h * cdf).astype(BF16)
    slope = cdf + h * jnp.exp(-0.5 * h * h) * (1.0 / math.sqrt(2.0 * math.pi))
    gs[0] = g
    ts[0] = slope.astype(BF16)
    acc[...] += dot_nn(g, w2[...])

    @pl.when(step == pl.num_programs(0) - 1)
    def _():
        m = acc[...] + c2[...]
        ms[0] = m
        x1 = x[0].astype(F32) + s1[...] * att[0]
        y = ((x1 + s2[...] * m) * row_valid(sc)).astype(BF16)
        ys[0] = y
        sent[...] = y


FF_CHUNK = 512


def mlp_fwd(sc, saved, vec, w1, w2, bufs):
    d, ff = w1.shape
    n = PIECES + 1
    xs, atts, bs = saved
    whole = pl.BlockSpec((1, d), lambda i, s: (0, 0))
    slot = lambda i, s: (s[0], 0, 0)
    chunk = lambda i, s: (s[0], 0, i)
    args = [xs, atts, bs, w1, vec["c1"], w2, vec["c2"], vec["s1"], vec["s2"]]
    in_specs = [
        pl.BlockSpec((1, HALF, d), slot),
        pl.BlockSpec((1, HALF, d), slot),
        pl.BlockSpec((1, HALF, d), slot),
        pl.BlockSpec((d, FF_CHUNK), lambda i, s: (0, i)),
        pl.BlockSpec((1, FF_CHUNK), lambda i, s: (0, i)),
        pl.BlockSpec((FF_CHUNK, d), lambda i, s: (i, 0)),
        whole,
        whole,
        whole,
    ]
    alias = {}
    if bufs is not None:
        alias = {1 + len(args) + j: j for j in range(len(bufs))}
        args = args + list(bufs)
        in_specs = in_specs + [pl.BlockSpec(memory_space=pl.ANY)] * len(bufs)
    outs = pl.pallas_call(
        mlp_fwd_body,
        out_shape=[
            jax.ShapeDtypeStruct((n, HALF, ff), BF16),
            jax.ShapeDtypeStruct((n, HALF, ff), BF16),
            jax.ShapeDtypeStruct((n, HALF, d), F32),
            jax.ShapeDtypeStruct((n, HALF, d), BF16),
            jax.ShapeDtypeStruct((HALF, d), BF16),
        ],
        grid_spec=pltpu.PrefetchScalarGridSpec(
            num_scalar_prefetch=1,
            grid=(ff // FF_CHUNK,),
            in_specs=in_specs,
            out_specs=[
                pl.BlockSpec((1, HALF, FF_CHUNK), chunk),
                pl.BlockSpec((1, HALF, FF_CHUNK), chunk),
                pl.BlockSpec((1, HALF, d), slot),
                pl.BlockSpec((1, HALF, d), slot),
                pl.BlockSpec((HALF, d), lambda i, s: (0, 0)),
            ],
            scratch_shapes=[pltpu.VMEM((HALF, d), F32)],
        ),
        compiler_params=params(),
        input_output_aliases=alias,
        name="mlp_fwd",
        cost_estimate=cost(11.5),
    )(sc, *args)
    return outs[:4], outs[4]


def incoming_rows(sc, cot, arr):
    dy = jnp.where(sc[2] == 0, arr[...], cot[0]).astype(F32)
    return dy * row_valid(sc)


def mlp_bwd_body(sc, cot, arr, x, att, m, slope, w1, w2, wo, s1, s2, g2, *rest):
    dms, dhs, d1s, das, dos, vecs, hbs = rest[-9:-2]
    dm_s, acc = rest[-2:]
    step = pl.program_id(0)

    @pl.when(step == 0)
    def _():
        dyv = incoming_rows(sc, cot, arr)
        d1s[0] = dyv
        dm = (s2[...] * dyv).astype(BF16)
        dm_s[...] = dm
        dms[0] = dm
        acc[...] = jnp.zeros_like(acc)
        vecs[0, 4:5] = col_sum(dm.astype(F32))
        vecs[0, 5:6] = col_sum(dyv * m[0])
        vecs[0, 6:8] = jnp.zeros_like(vecs[0, 6:8])

    dh = (dot_nt(dm_s[...], w2[...]) * slope[0].astype(F32)).astype(BF16)
    dhs[0] = dh
    hbs[0] = jnp.broadcast_to(col_sum(dh.astype(F32)), hbs.shape[1:])
    acc[...] += dot_nt(dh, w1[...])

    @pl.when(step == pl.num_programs(0) - 1)
    def _():
        x1 = x[0].astype(F32) + s1[...] * att[0]
        standard, inverse = standardise(x1)
        db = acc[...]
        dx1 = d1s[0] + norm_back(db, standard, inverse, g2[...])
        d1s[0] = dx1
        da = (s1[...] * dx1).astype(BF16)
        das[0] = da
        vecs[0, 0:1] = col_sum(da.astype(F32))
        vecs[0, 1:2] = col_sum(dx1 * att[0])
        vecs[0, 2:3] = col_sum(db * standard)
        vecs[0, 3:4] = col_sum(db)
        dos[0] = dot_nt(da, wo[...]).astype(BF16)


def mlp_bwd(sc, cot, arr, saved, vec, w1, w2, wo, bufs):
    d, ff = w1.shape
    n = PIECES + 1
    xs, atts, ms, ts = saved
    whole = pl.BlockSpec((1, d), lambda i, s: (0, 0))
    slot = lambda i, s: (s[0], 0, 0)
    read = lambda i, s: (s[1], 0, 0)
    chunk = lambda i, s: (s[0], 0, i)
    args = [cot, arr, xs, atts, ms, ts, w1, w2, wo, vec["s1"], vec["s2"], vec["g2"]]
    in_specs = [
        pl.BlockSpec((1, HALF, d), read),
        pl.BlockSpec((HALF, d), lambda i, s: (0, 0)),
        pl.BlockSpec((1, HALF, d), read),
        pl.BlockSpec((1, HALF, d), read),
        pl.BlockSpec((1, HALF, d), read),
        pl.BlockSpec((1, HALF, FF_CHUNK), lambda i, s: (s[1], 0, i)),
        pl.BlockSpec((d, FF_CHUNK), lambda i, s: (0, i)),
        pl.BlockSpec((FF_CHUNK, d), lambda i, s: (i, 0)),
        pl.BlockSpec((d, d), lambda i, s: (0, 0)),
        whole,
        whole,
        whole,
    ]
    alias = {}
    if bufs is not None:
        alias = {1 + len(args) + j: j for j in range(len(bufs))}
        args = args + list(bufs)
        in_specs = in_specs + [pl.BlockSpec(memory_space=pl.ANY)] * len(bufs)
    return pl.pallas_call(
        mlp_bwd_body,
        out_shape=[
            jax.ShapeDtypeStruct((n, HALF, d), BF16),
            jax.ShapeDtypeStruct((n, HALF, ff), BF16),
            jax.ShapeDtypeStruct((n, HALF, d), F32),
            jax.ShapeDtypeStruct((n, HALF, d), BF16),
            jax.ShapeDtypeStruct((n, HALF, d), BF16),
            jax.ShapeDtypeStruct((n, 8, d), F32),
            jax.ShapeDtypeStruct((n, 8, ff), F32),
        ],
        grid_spec=pltpu.PrefetchScalarGridSpec(
            num_scalar_prefetch=1,
            grid=(ff // FF_CHUNK,),
            in_specs=in_specs,
            out_specs=[
                pl.BlockSpec((1, HALF, d), slot),
                pl.BlockSpec((1, HALF, FF_CHUNK), chunk),
                pl.BlockSpec((1, HALF, d), slot),
                pl.BlockSpec((1, HALF, d), slot),
                pl.BlockSpec((1, HALF, d), slot),
                pl.BlockSpec((1, 8, d), slot),
                pl.BlockSpec((1, 8, FF_CHUNK), chunk),
            ],
            scratch_shapes=[pltpu.VMEM((HALF, d), BF16), pltpu.VMEM((HALF, d), F32)],
        ),
        compiler_params=params(),
        input_output_aliases=alias,
        name="mlp_bwd",
        cost_estimate=cost(14),
    )(sc, *args)


def attn_bwd_body(first, sc, x, d1, q, k, v, do, pg, plc, wq, wk, wv, g1, b1, *rest):
    dqs, dks, dvs, dxs, as_, vecs, bvs, dgs, sent = rest[-10:-1]
    acc = rest[-1]
    old = None if first else rest[0]
    step = pl.program_id(0)

    @pl.when(step == 0)
    def _():
        acc[...] = jnp.zeros_like(acc)

    zero = jnp.zeros((HALF, 128), BF16)
    for pair in range(2):
        lanes = slice(pair * 128, pair * 128 + 128)
        qp, kp, vp, dp_ = q[0, :, lanes], k[0, :, lanes], v[0, :, lanes], do[0, :, lanes]
        total = [None] * 9
        for hh in range(2):
            head = pair * 2 + hh
            mask = half_mask((HALF, 128), hh)
            qm = jnp.where(mask, qp, zero)
            km = jnp.where(mask, kp, zero)
            vm = jnp.where(mask, vp, zero)
            dm = jnp.where(mask, dp_, zero)
            parts = []
            local = None
            for j in range(3):
                rows = slice(0, GPAD) if j == 0 else slice(GPAD + (j - 1) * LPAD, GPAD + j * LPAD)
                p = pg[0, head] if j == 0 else plc[0, head, j - 1]
                pb = p.astype(BF16)
                dp = dot_nt(dp_[rows], vm[rows])
                ds = (p * (dp - jnp.sum(dp * p, axis=-1, keepdims=True))).astype(BF16)
                if j == 0:
                    dg = ds.astype(F32)
                    dgs[0, head] = dg if first else jnp.where(sc[4] == 1, dg, old[0, head] + dg)
                else:
                    local = ds.astype(F32) if local is None else local + ds.astype(F32)
                parts += [dot_nn(ds, km[rows]), dot_tn(ds, qm[rows]), dot_tn(pb, dm[rows])]
            dgs[0, head, :LPAD, :LPAD] += local
            total = [b if a is None else a + b for a, b in zip(total, parts)]
        for j in range(3):
            rows = slice(0, GPAD) if j == 0 else slice(GPAD + (j - 1) * LPAD, GPAD + j * LPAD)
            dqs[0, rows, lanes] = total[3 * j].astype(BF16) * HEAD_DIM ** (-0.5)
            dks[0, rows, lanes] = total[3 * j + 1].astype(BF16)
            dvs[0, rows, lanes] = total[3 * j + 2].astype(BF16)
    dq, dk, dv = dqs[0], dks[0], dvs[0]
    bvs[0, 0:1] = col_sum(dq.astype(F32))
    bvs[0, 1:2] = col_sum(dv.astype(F32))
    bvs[0, 2:8] = jnp.zeros_like(bvs[0, 2:8])
    acc[...] += dot_nt(dq, wq[...]) + dot_nt(dk, wk[...]) + dot_nt(dv, wv[...])

    @pl.when(step == pl.num_programs(0) - 1)
    def _():
        standard, inverse = standardise(x[0].astype(F32))
        as_[0] = (standard * g1[...] + b1[...]).astype(BF16)
        da = acc[...]
        dx = (d1[0] + norm_back(da, standard, inverse, g1[...])).astype(BF16)
        dxs[0] = dx
        sent[...] = dx
        vecs[0, 0:1] = col_sum(da * standard)
        vecs[0, 1:2] = col_sum(da)
        vecs[0, 2:8] = jnp.zeros_like(vecs[0, 2:8])


def attn_bwd(sc, saved, vec, wa, bufs, dgrid):
    xs, d1s, qs, ks, vs, dos, pgs, pls = saved
    d = xs.shape[-1]
    heads = pgs.shape[1]
    groups = d // 256
    per = heads // groups
    n = PIECES + 1
    whole = pl.BlockSpec((1, d), lambda i, s: (0, 0))
    slot = lambda i, s: (s[0], 0, 0)
    read = lambda i, s: (s[1], 0, 0)
    now = lambda i, s: (s[0], 0, 0)
    chunk = lambda i, s: (s[0], 0, i)
    first = dgrid is None
    rchunk = pl.BlockSpec((1, HALF, 256), lambda i, s: (s[1], 0, i))
    grid_spec = pl.BlockSpec((1, per, GPAD, GPAD), lambda i, s: (s[3], i, 0, 0))
    args = [xs, d1s, qs, ks, vs, dos, pgs, pls, wa, wa, wa, vec["g1"], vec["b1"]]
    in_specs = [
        pl.BlockSpec((1, HALF, d), read),
        pl.BlockSpec((1, HALF, d), now),
        rchunk,
        rchunk,
        rchunk,
        pl.BlockSpec((1, HALF, 256), chunk),
        pl.BlockSpec((1, per, GPAD, GPAD), lambda i, s: (s[1], i, 0, 0)),
        pl.BlockSpec((1, per, 2, LPAD, LPAD), lambda i, s: (s[1], i, 0, 0, 0)),
        pl.BlockSpec((d, 256), lambda i, s: (0, i)),
        pl.BlockSpec((d, 256), lambda i, s: (0, groups + i)),
        pl.BlockSpec((d, 256), lambda i, s: (0, 2 * groups + i)),
        whole,
        whole,
    ]
    alias = {}
    if not first:
        alias[1 + len(args)] = 7
        args = args + [dgrid]
        in_specs = in_specs + [grid_spec]
        for j in range(len(bufs)):
            alias[1 + len(args) + j] = j
        args = args + list(bufs)
        in_specs = in_specs + [pl.BlockSpec(memory_space=pl.ANY)] * len(bufs)
    outs = pl.pallas_call(
        functools.partial(attn_bwd_body, first),
        out_shape=[
            jax.ShapeDtypeStruct((n, HALF, d), BF16),
            jax.ShapeDtypeStruct((n, HALF, d), BF16),
            jax.ShapeDtypeStruct((n, HALF, d), BF16),
            jax.ShapeDtypeStruct((n, HALF, d), BF16),
            jax.ShapeDtypeStruct((n, HALF, d), BF16),
            jax.ShapeDtypeStruct((n, 8, d), F32),
            jax.ShapeDtypeStruct((n, 8, d), F32),
            jax.ShapeDtypeStruct((2, heads, GPAD, GPAD), F32),
            jax.ShapeDtypeStruct((HALF, d), BF16),
        ],
        grid_spec=pltpu.PrefetchScalarGridSpec(
            num_scalar_prefetch=1,
            grid=(groups,),
            in_specs=in_specs,
            out_specs=[
                pl.BlockSpec((1, HALF, 256), chunk),
                pl.BlockSpec((1, HALF, 256), chunk),
                pl.BlockSpec((1, HALF, 256), chunk),
                pl.BlockSpec((1, HALF, d), slot),
                pl.BlockSpec((1, HALF, d), slot),
                pl.BlockSpec((1, 8, d), slot),
                pl.BlockSpec((1, 8, 256), chunk),
                grid_spec,
                pl.BlockSpec((HALF, d), lambda i, s: (0, 0)),
            ],
            scratch_shapes=[pltpu.VMEM((HALF, d), F32)],
        ),
        compiler_params=params(),
        input_output_aliases=alias,
        name="attn_bwd",
        cost_estimate=cost(15.5),
    )(sc, *args)
    return outs[:7], outs[7], outs[8]


def weight_body(pairs, last, sc, *refs):
    lefts, rights = refs[:pairs], refs[pairs : 2 * pairs]
    refs = refs[2 * pairs :]
    if last:
        arr, scale = refs[:2]
        refs = refs[2:]
    keep, send = refs[:2]
    step = pl.program_id(0)
    half = pl.num_programs(0) // 2
    rows = PIECES * HALF
    if last:
        dm_s = refs[2]

        @pl.when(step == 0)
        def _():
            for p in range(PIECES - 1):
                dm_s[p * HALF : (p + 1) * HALF] = rights[0][p]
            dy = arr[...].astype(F32) * row_valid(sc)
            fresh = (scale[...] * dy).astype(BF16)
            dm_s[rows - HALF : rows] = jnp.where(sc[2] == 0, fresh, rights[0][PIECES - 1])

    parts = []
    for left, right in zip(lefts, rights):
        a = left[...].reshape(rows, left.shape[2])
        b = dm_s[...] if last else right[...].reshape(rows, right.shape[2])
        parts.append(dot_tn(a, b).astype(BF16))

    @pl.when(step < half)
    def _():
        for j, part in enumerate(parts):
            send[:, j * part.shape[1] : (j + 1) * part.shape[1]] = part

    @pl.when(step >= half)
    def _():
        for j, part in enumerate(parts):
            keep[:, j * part.shape[1] : (j + 1) * part.shape[1]] = part


def weight_grad(sc, pairs, rows, block, us, last=None, columns=None):
    offset, count = rows
    half = count // 2 // block
    assert half * 2 * block == count and offset % block == 0
    first = offset // block

    def source(i, s):
        other = jnp.where(i < half, 1 - s[8], s[8])
        return first + other * half + jnp.where(i < half, i, i - half)

    begin, wide = columns or (0, pairs[0][1].shape[2])
    assert begin % wide == 0
    width = wide * len(pairs)
    in_specs = [
        pl.BlockSpec((PIECES, HALF, block), lambda i, s: (0, 0, source(i, s))) for _ in pairs
    ] + [
        pl.BlockSpec((PIECES, HALF, wide), lambda i, s: (0, 0, begin // wide)) for _ in pairs
    ]
    args = [left for left, _ in pairs] + [right for _, right in pairs]
    scratch = []
    if last is not None:
        d = last[0].shape[1]
        in_specs += [
            pl.BlockSpec((HALF, d), lambda i, s: (0, 0)),
            pl.BlockSpec((1, d), lambda i, s: (0, 0)),
        ]
        args += list(last)
        scratch = [pltpu.VMEM((PIECES * HALF, d), BF16)]
    return pl.pallas_call(
        functools.partial(weight_body, len(pairs), last is not None),
        out_shape=[jax.ShapeDtypeStruct((count // 2, width), BF16)] * 2,
        grid_spec=pltpu.PrefetchScalarGridSpec(
            num_scalar_prefetch=1,
            grid=(2 * half,),
            in_specs=in_specs,
            out_specs=[
                pl.BlockSpec((block, width), lambda i, s: (jnp.maximum(i - half, 0), 0)),
                pl.BlockSpec((block, width), lambda i, s: (jnp.minimum(i, half - 1), 0)),
            ],
            scratch_shapes=scratch,
        ),
        compiler_params=params(),
        cost_estimate=cost(us),
        name="weight_grad",
    )(sc, *args)


TABLE = 768
INNER = 256
OUTER = TABLE // INNER
ROWS = 16


def one_hot(index_row):
    outer = lax.shift_right_logical(index_row, 8)
    inner = index_row - outer * INNER
    high = lax.shift_right_logical(inner, 4)
    low = inner - high * 16
    rows = lax.broadcasted_iota(jnp.int32, (16, GPAD), 0)
    block = jnp.where(rows == low, 1.0, 0.0).astype(BF16)
    which = jnp.broadcast_to(high.astype(F32), (16, GPAD)).astype(BF16)
    zero = jnp.zeros((16, GPAD), BF16)
    hot = [jnp.where(which == jnp.bfloat16(a), block, zero) for a in range(INNER // 16)]
    return jnp.concatenate(hot, axis=0), outer


def grid_body(table, index, out):
    heads = out.shape[0]
    column = lax.broadcasted_iota(jnp.int32, (16, GPAD), 1)
    for r in range(ROWS):
        hot, outer = one_hot(index[r : r + 1, :])
        parts = dot_nn(table[...], hot)
        values = jnp.zeros((16, GPAD), F32)
        for a in range(OUTER):
            own = parts[a * 32 : a * 32 + 16] + parts[a * 32 + 16 : a * 32 + 32]
            values = jnp.where(outer == a, own, values)
        values = jnp.where(column < GLOB, values, NEGATIVE)
        for h in range(heads):
            out[h, r : r + 1, :] = values[h : h + 1]


def build_grid(table, index):
    rows, heads = table.shape
    flat = jnp.pad(table.T, ((0, 16 - heads), (0, TABLE - rows)))
    high = flat.astype(BF16)
    low = (flat - high.astype(F32)).astype(BF16)
    stacked = jnp.concatenate(
        [part[:, a * INNER : (a + 1) * INNER] for a in range(OUTER) for part in (high, low)], axis=0
    )
    return pl.pallas_call(
        grid_body,
        out_shape=jax.ShapeDtypeStruct((heads, GPAD, GPAD), F32),
        grid=(GPAD // ROWS,),
        in_specs=[
            pl.BlockSpec((32 * OUTER, INNER), lambda i: (0, 0)),
            pl.BlockSpec((ROWS, GPAD), lambda i: (i, 0)),
        ],
        out_specs=pl.BlockSpec((heads, ROWS, GPAD), lambda i: (0, i, 0)),
        compiler_params=params(),
        name="build_grid",
        cost_estimate=cost(8),
    )(stacked, index)


def table_body(sc, index, dg, out):
    step = pl.program_id(0)
    heads = dg.shape[1]

    @pl.when(step == 0)
    def _():
        out[...] = jnp.zeros_like(out)

    total = jnp.zeros((32 * OUTER, INNER), F32)
    pad = jnp.zeros((16 - heads, GPAD), F32)
    for r in range(ROWS):
        hot, outer = one_hot(index[r : r + 1, :])
        rows = jnp.concatenate([dg[0, h, r : r + 1, :] for h in range(heads)] + [pad], axis=0)
        high = rows.astype(BF16).astype(F32)
        both = jnp.concatenate([high, rows - high], axis=0)
        left = jnp.concatenate([jnp.where(outer == a, both, 0.0) for a in range(OUTER)], axis=0)
        total += dot_nt(left.astype(BF16), hot)
    out[...] += total


def table_grad(sc, index, dgrid):
    heads = dgrid.shape[1]
    out = pl.pallas_call(
        table_body,
        out_shape=jax.ShapeDtypeStruct((32 * OUTER, INNER), F32),
        grid_spec=pltpu.PrefetchScalarGridSpec(
            num_scalar_prefetch=1,
            grid=(GPAD // ROWS,),
            in_specs=[
                pl.BlockSpec((ROWS, GPAD), lambda i, s: (i, 0)),
                pl.BlockSpec((1, heads, ROWS, GPAD), lambda i, s: (0, 0, i, 0)),
            ],
            out_specs=pl.BlockSpec((32 * OUTER, INNER), lambda i, s: (0, 0)),
        ),
        compiler_params=params(),
        name="table_grad",
        cost_estimate=cost(18),
    )(sc, index, dgrid)
    parts = [out[a * 32 : a * 32 + 16] + out[a * 32 + 16 : a * 32 + 32] for a in range(OUTER)]
    return jnp.concatenate(parts, axis=1)


def unpack_body(pieces, out):
    a, b = pieces[0].astype(F32), pieces[1].astype(F32)
    parts = [a[:GLOB], b[:GLOB]]
    for half in (a, b):
        for j in range(2):
            parts.append(half[GPAD + j * LPAD : GPAD + j * LPAD + LOC])
    tail = out.shape[1] - 2 * GLOB - 4 * LOC
    parts.append(jnp.zeros((tail, a.shape[1]), F32))
    out[0] = jnp.concatenate(parts, axis=0).astype(BF16)


def unpack(pieces, slot_rows):
    d = pieces.shape[2]
    return pl.pallas_call(
        unpack_body,
        out_shape=jax.ShapeDtypeStruct((PIECES // 2, slot_rows, d), BF16),
        grid=(PIECES // 2,),
        in_specs=[pl.BlockSpec((2, HALF, d), lambda i: (i, 0, 0))],
        out_specs=pl.BlockSpec((1, slot_rows, d), lambda i: (i, 0, 0)),
        compiler_params=params(),
        cost_estimate=cost(3),
        name="unpack",
    )(pieces)


def pack(rows):
    pieces = []
    for m in range(rows.shape[0]):
        for u in range(2):
            own = rows[m]
            parts = [jnp.pad(own[u * GLOB : (u + 1) * GLOB], ((0, GPAD - GLOB), (0, 0)))]
            for j in range(2):
                begin = 2 * GLOB + (2 * u + j) * LOC
                parts.append(jnp.pad(own[begin : begin + LOC], ((0, LPAD - LOC), (0, 0))))
            pieces.append(jnp.concatenate(parts, axis=0))
    return jnp.stack(pieces)


def exchange(value, bit):
    peers = lax.axis_size("dp")
    return lax.ppermute(value, "dp", [(i, i ^ (1 << bit)) for i in range(peers)])


def own_bit(bit):
    return (lax.axis_index("dp") >> bit) & 1


class Small:
    def __init__(self, value, order):
        self.value = value
        self.left = list(order)
        self.done = False

    def begin(self):
        return exchange(self.value, self.left[0])

    def finish(self, got):
        self.value = self.value + got
        self.left = self.left[1:]
        self.done = not self.left


class Job:
    def __init__(self, parts, order):
        self.keep, self.send = parts
        self.order = order
        self.place = 0
        self.back = False
        self.done = False

    def begin(self):
        bit = self.order[self.place]
        return exchange(self.keep if self.back else self.send, bit)

    def finish(self, got):
        bit = self.order[self.place]
        if self.back:
            part = self.keep
            self.keep = jnp.where(
                own_bit(bit) == 0,
                jnp.concatenate([part, got], axis=0),
                jnp.concatenate([got, part], axis=0),
            )
            self.place -= 1
            self.done = self.place < 0
            return
        if self.place + 1 == len(self.order):
            self.keep = (self.keep.astype(F32) + got.astype(F32)).astype(BF16)
            self.back = True
            return
        half = self.keep.shape[0] // 2
        following = own_bit(self.order[self.place + 1])
        keep = self.keep

        def part(side):
            a = lax.dynamic_slice_in_dim(keep, side * half, half, 0)
            b = lax.dynamic_slice_in_dim(got, side * half, half, 0)
            return (a.astype(F32) + b.astype(F32)).astype(BF16)

        self.keep, self.send = part(following), part(1 - following)
        self.place += 1


def advance(gate, jobs):
    gate, *got = lax.optimization_barrier((gate, *[job.begin() for job in jobs]))
    for job, value in zip(jobs, got):
        job.finish(value)
    return gate


def body(
    tokens,
    cotangent,
    crop_lengths,
    relative_index,
    first_gain,
    first_shift,
    attend_weight,
    query_bias,
    value_bias,
    relative_table,
    output_weight,
    output_bias,
    scale_one,
    second_gain,
    second_shift,
    expand_weight,
    expand_bias,
    reduce_weight,
    reduce_bias,
    scale_two,
):
    micro, slot_rows, d = tokens.shape
    assert micro * 2 == PIECES and crop_lengths.shape[1] == 1
    pipe = lax.axis_index("pipe")
    vec = dict(
        g1=first_gain, b1=first_shift, bq=query_bias, bv=value_bias, bo=output_bias,
        s1=scale_one, g2=second_gain, b2=second_shift, c1=expand_bias, c2=reduce_bias, s2=scale_two,
    )
    wa, wo, w1, w2 = attend_weight[0], output_weight[0], expand_weight[0], reduce_weight[0]
    table = relative_table[0]
    index = jnp.pad(relative_index, ((0, GPAD - GLOB), (0, GPAD - GLOB)))
    tok, cot = pack(tokens), pack(cotangent)
    grid = build_grid(table, index)
    blank = jnp.zeros((HALF, d), BF16)
    own = crop_lengths[:, 0, :]
    lengths = jnp.concatenate([own[:, :1], own[:, 2:4], own[:, 1:2], own[:, 4:6]], axis=1)
    lengths = lengths.reshape(PIECES, 3)

    def scalars(mine):
        active = jnp.logical_and(mine >= 0, mine < PIECES)
        read = jnp.clip(mine, 0, PIECES - 1)
        pick = (read[:, None] == jnp.arange(PIECES)[None, :]).astype(jnp.int32)
        crops = jnp.sum(pick[:, :, None] * lengths[None], axis=1)
        ones = jnp.ones_like(mine)
        columns = [
            jnp.where(active, mine, PIECES), read, ones * pipe, jnp.where(active, 0, 1),
            jnp.where(mine == 0, 1, 0), crops[:, 0], crops[:, 1], crops[:, 2], ones * own_bit(0),
        ]
        return jnp.stack(columns, axis=1).astype(jnp.int32)

    lag = 2
    steps = PIECES + lag
    moments = jnp.arange(steps, dtype=jnp.int32)
    ahead = scalars(moments - lag * pipe)
    behind = scalars(moments - lag * (1 - pipe))
    attn = mlp = None
    moving = []
    for t in range(steps):
        sc = ahead[t]
        arr = moving[t - lag] if t >= lag else blank
        attn = attn_fwd(sc, tok, arr, vec, wa, wo, grid, attn)
        mlp, sent = mlp_fwd(sc, (attn[0], attn[7], attn[8]), vec, w1, w2, mlp)
        if t < PIECES:
            moving.append(lax.ppermute(sent, "pipe", [(0, 1)]))
    xs, qs, ks, vs, pgs, pls, os_, atts, bs = attn
    gs, ts, ms, ys = mlp
    ff = w1.shape[1]
    first = second = dgrid = None
    moving = []
    bits = lax.axis_size("dp").bit_length() - 1
    plain = list(range(bits))
    other = [plain[0], plain[2], plain[1]] + plain[3:]
    for t in range(steps):
        sc = behind[t]
        arr = moving[t - lag] if t >= lag else blank
        final = t == steps - 1
        if final:
            sc = behind_last
        first = mlp_bwd(sc, cot, arr, (xs, atts, ms, ts), vec, w1, w2, wo, first)
        if t == steps - 2:
            last = (moving[t + 1 - lag], vec["s2"])
            a, b = [
                Job(
                    weight_grad(
                        behind[t + 1], [(gs, first[0])], (r * ff // 2, ff // 2), 384, 8, last
                    ),
                    plain,
                )
                for r in range(2)
            ]
            sc, b.keep, b.send = lax.optimization_barrier((sc, b.keep, b.send))
            sc = advance(sc, [a])
        if final:
            sc = advance(sc, [a, b])
            c, e = [
                Job(
                    weight_grad(
                        sc, [(bs, first[1])], (0, d), 128, 7, columns=(r * ff // 2, ff // 2)
                    ),
                    order,
                )
                for r, order in enumerate((plain, other))
            ]
            sc = advance(sc, [a, b])
        second, dgrid, sent = attn_bwd(
            sc, (xs, first[2], qs, ks, vs, first[4], pgs, pls), vec, wa, second, dgrid
        )
        if t == steps - 2:
            behind_last = advance(behind[t + 1], [a, b])
        if t < PIECES:
            moving.append(lax.ppermute(sent, "pipe", [(1, 0)]))
    dms, dhs, d1s, das, dos, late, late_bias = first
    dqs, dks, dvs, dxs, as_, early, early_bias = second

    sc = advance(sc, [a, b, c, e])
    q = Job(weight_grad(sc, [(os_, das), (as_, dqs)], (0, d), 384, 9), plain)
    k = Job(weight_grad(sc, [(as_, dks), (as_, dvs)], (0, d), 384, 9), plain)
    sc = advance(sc, [a, b, c])
    d_table = table_grad(sc, index, dgrid)
    small = jnp.concatenate(
        [
            jnp.sum(late[:PIECES, :6], axis=0).reshape(-1),
            jnp.sum(early[:PIECES, :2], axis=0).reshape(-1),
            jnp.sum(early_bias[:PIECES, :2], axis=0).reshape(-1),
            jnp.sum(late_bias[:PIECES, 0], axis=0),
            d_table.reshape(-1),
        ]
    ).reshape(-1, d)
    s = Small(small, plain)
    tail = [[c, e, a, q, k], [q, e, c, b, a], [k, q, c, e, s], [b, k, q, e, s], [e, c, k, q, b, s]]
    tail += [[c, k, q, s], [q, k, c], [k, e, q], [k, e]]
    for jobs in tail:
        sc = advance(sc, [job for job in jobs if not job.done])
    everything = [a, b, c, e, q, k, s]
    while not all(job.done for job in everything):
        sc = advance(sc, [job for job in everything if not job.done])
    small = s.value
    whole = [job.keep.astype(F32) for job in (a, b, c, e, q, k)]
    reduce_grad = jnp.concatenate(whole[:2], axis=0)
    expand_grad = jnp.concatenate(whole[2:4], axis=1)
    output_grad = whole[4][:, :d]
    attend_grad = jnp.concatenate([whole[4][:, d:], whole[5]], axis=1)
    expand_bias_grad = small[10 : 10 + ff // d].reshape(-1)
    table_sum = small[10 + ff // d :].reshape(16, -1)[: table.shape[1], : table.shape[0]].T
    ordered = (
        small[6], small[7], attend_grad, small[8], small[9], table_sum, output_grad,
        small[0], small[1], small[2], small[3], expand_grad, expand_bias_grad, reduce_grad,
        small[4], small[5],
    )
    outputs = unpack(ys, slot_rows)
    grads = unpack(dxs, slot_rows)
    return (outputs[None], grads[None]) + tuple(member[None] for member in ordered)


def solution(mesh):
    in_specs = (
        P(None, "dp", None),
        P(None, "dp", None),
        P(None, "dp", None),
        P(),
        P("pipe", None),
        P("pipe", None),
        P("pipe", None, None),
        P("pipe", None),
        P("pipe", None),
        P("pipe", None, None),
        P("pipe", None, None),
        P("pipe", None),
        P("pipe", None),
        P("pipe", None),
        P("pipe", None),
        P("pipe", None, None),
        P("pipe", None),
        P("pipe", None, None),
        P("pipe", None),
        P("pipe", None),
    )
    out_specs = (
        P("pipe", None, "dp", None),
        P("pipe", None, "dp", None),
        P("pipe", None),
        P("pipe", None),
        P("pipe", None, None),
        P("pipe", None),
        P("pipe", None),
        P("pipe", None, None),
        P("pipe", None, None),
        P("pipe", None),
        P("pipe", None),
        P("pipe", None),
        P("pipe", None),
        P("pipe", None, None),
        P("pipe", None),
        P("pipe", None, None),
        P("pipe", None),
        P("pipe", None),
    )
    return jax.shard_map(body, mesh=mesh, in_specs=in_specs, out_specs=out_specs, check_vma=False)
```

```python
import functools
import math

import jax
import jax.numpy as jnp
from jax import lax
from jax.experimental import pallas as pl
from jax.experimental.pallas import tpu as pltpu
from jax.sharding import PartitionSpec as P

F32 = jnp.float32
BF16 = jnp.bfloat16
EPSILON = 1e-06
HEAD_DIM = 64
GLOB = 197
LOC = 36
GPAD = 208
LPAD = 48
HALF = GPAD + 2 * LPAD
SPAN = 2 * HALF
PIECES = 2
BLOCKS = tuple(
    block
    for u in range(2)
    for block in (
        (True, u, u * HALF, GPAD),
        (False, 2 * u, u * HALF + GPAD, LPAD),
        (False, 2 * u + 1, u * HALF + GPAD + LPAD, LPAD),
    )
)
NEGATIVE = -1e30
VMEM_LIMIT = 56 * 1024 * 1024


def dot_nn(a, b):
    return jnp.dot(a, b, preferred_element_type=F32)


def dot_nt(a, b):
    return lax.dot_general(a, b, (((1,), (1,)), ((), ())), preferred_element_type=F32)


def dot_tn(a, b):
    return lax.dot_general(a, b, (((0,), (0,)), ((), ())), preferred_element_type=F32)


def standardise(values):
    average = jnp.mean(values, axis=-1, keepdims=True)
    centred = values - average
    inverse = lax.rsqrt(jnp.mean(centred * centred, axis=-1, keepdims=True) + EPSILON)
    return centred * inverse, inverse


def norm_back(incoming, standard, inverse, gain):
    scaled = incoming * gain
    return inverse * (
        scaled
        - jnp.mean(scaled, axis=-1, keepdims=True)
        - standard * jnp.mean(scaled * standard, axis=-1, keepdims=True)
    )


def col_sum(values):
    return jnp.sum(values, axis=0, keepdims=True)


def params(n=1):
    return pltpu.CompilerParams(
        dimension_semantics=("arbitrary",) * n, vmem_limit_bytes=VMEM_LIMIT
    )


def row_valid(sc):
    row = lax.broadcasted_iota(jnp.int32, (SPAN, 1), 0)
    limit = BLOCKS[0][2] + sc[5]
    for j, (_, _, begin, _) in enumerate(BLOCKS[1:], 1):
        limit = jnp.where(row < begin, limit, begin + sc[5 + j])
    return jnp.where(row < limit, 1.0, 0.0)


def cost(us):
    return pl.CostEstimate(flops=int(us * 1.1e9), bytes_accessed=int(us * 1e6), transcendentals=0)


def skipping(inner, sc, *refs):
    @pl.when(sc[11] == 1)
    def _():
        inner(sc, *refs)


def half_mask(shape, which):
    lane = lax.broadcasted_iota(jnp.int32, shape, 1)
    return (lane < HEAD_DIM) if which == 0 else (lane >= HEAD_DIM)


def attn_fwd_body(sc, tok, arr, g1, b1, wq, wk, wv, bq, bv, wo, grid, bo, s1, g2, b2, *rest):
    outs = rest[len(rest) - 2 - 9 : len(rest) - 2]
    xs, qs, ks, vs, pgs, pls, os_, atts, bs = outs
    a_s, acc = rest[-2:]
    step = pl.program_id(0)

    @pl.when(step == 0)
    def _():
        x = jnp.where(sc[2] == 0, tok[0], arr[...])
        xs[0] = x
        standard, _ = standardise(x.astype(F32))
        a_s[...] = (standard * g1[...] + b1[...]).astype(BF16)
        acc[...] = jnp.zeros_like(acc)

    a = a_s[...]
    q = ((dot_nn(a, wq[...]) + bq[...]) * HEAD_DIM ** (-0.5)).astype(BF16)
    k = dot_nn(a, wk[...]).astype(BF16)
    v = (dot_nn(a, wv[...]) + bv[...]).astype(BF16)
    qs[0] = q
    ks[0] = k
    vs[0] = v
    zero = jnp.zeros((SPAN, 128), BF16)
    for pair in range(2):
        lanes = slice(pair * 128, pair * 128 + 128)
        qp, kp, vp = q[:, lanes], k[:, lanes], v[:, lanes]
        total = [None] * len(BLOCKS)
        for hh in range(2):
            head = pair * 2 + hh
            mask = half_mask((SPAN, 128), hh)
            km = jnp.where(mask, kp, zero)
            vm = jnp.where(mask, vp, zero)
            column = lax.broadcasted_iota(jnp.int32, (LPAD, LPAD), 1)
            bias = jnp.where(column < LOC, grid[head, :LPAD, :LPAD], NEGATIVE)
            for n, (glob, j, begin, size) in enumerate(BLOCKS):
                rows = slice(begin, begin + size)
                s = dot_nt(qp[rows], km[rows]) + (grid[head] if glob else bias)
                e = jnp.exp(s - jnp.max(s, axis=-1, keepdims=True))
                p = e * (1.0 / jnp.sum(e, axis=-1, keepdims=True))
                kept = pgs if glob else pls
                kept[0, head, j] = p
                o = dot_nn(p.astype(BF16), vm[rows])
                total[n] = o if total[n] is None else total[n] + o
        for n, (_, _, begin, size) in enumerate(BLOCKS):
            os_[0, begin : begin + size, lanes] = total[n].astype(BF16)
    acc[...] += dot_nn(os_[0], wo[...])

    @pl.when(step == pl.num_programs(0) - 1)
    def _():
        att = acc[...] + bo[...]
        atts[0] = att
        x1 = xs[0].astype(F32) + s1[...] * att
        standard, _ = standardise(x1)
        bs[0] = (standard * g2[...] + b2[...]).astype(BF16)


def attn_fwd(sc, tok, arr, vec, wa, wo, grid, bufs):
    d = wo.shape[0]
    heads = grid.shape[0]
    groups = d // 256
    per = heads // groups
    whole = pl.BlockSpec((1, d), lambda i, s: (0, 0))
    slot = lambda i, s: (s[0], 0, 0)
    chunk = lambda i, s: (s[0], 0, i * s[11])
    n = PIECES + 1
    shapes = [
        jax.ShapeDtypeStruct((n, SPAN, d), BF16),
        jax.ShapeDtypeStruct((n, SPAN, d), BF16),
        jax.ShapeDtypeStruct((n, SPAN, d), BF16),
        jax.ShapeDtypeStruct((n, SPAN, d), BF16),
        jax.ShapeDtypeStruct((n, heads, 2, GPAD, GPAD), F32),
        jax.ShapeDtypeStruct((n, heads, 4, LPAD, LPAD), F32),
        jax.ShapeDtypeStruct((n, SPAN, d), BF16),
        jax.ShapeDtypeStruct((n, SPAN, d), F32),
        jax.ShapeDtypeStruct((n, SPAN, d), BF16),
    ]
    out_specs = [
        pl.BlockSpec((1, SPAN, d), slot),
        pl.BlockSpec((1, SPAN, 256), chunk),
        pl.BlockSpec((1, SPAN, 256), chunk),
        pl.BlockSpec((1, SPAN, 256), chunk),
        pl.BlockSpec((1, per, 2, GPAD, GPAD), lambda i, s: (s[0], i * s[11], 0, 0, 0)),
        pl.BlockSpec((1, per, 4, LPAD, LPAD), lambda i, s: (s[0], i * s[11], 0, 0, 0)),
        pl.BlockSpec((1, SPAN, 256), chunk),
        pl.BlockSpec((1, SPAN, d), slot),
        pl.BlockSpec((1, SPAN, d), slot),
    ]
    in_specs = [
        pl.BlockSpec((1, SPAN, d), lambda i, s: (s[1], 0, 0)),
        pl.BlockSpec((SPAN, d), lambda i, s: (0, 0)),
        whole,
        whole,
        pl.BlockSpec((d, 256), lambda i, s: (0, i * s[11])),
        pl.BlockSpec((d, 256), lambda i, s: (0, groups + i * s[11])),
        pl.BlockSpec((d, 256), lambda i, s: (0, 2 * groups + i * s[11])),
        pl.BlockSpec((1, 256), lambda i, s: (0, i * s[11])),
        pl.BlockSpec((1, 256), lambda i, s: (0, i * s[11])),
        pl.BlockSpec((256, d), lambda i, s: (i * s[11], 0)),
        pl.BlockSpec((per, GPAD, GPAD), lambda i, s: (i * s[11], 0, 0)),
        whole,
        whole,
        whole,
        whole,
    ]
    args = [tok, arr, vec["g1"], vec["b1"], wa, wa, wa, vec["bq"], vec["bv"], wo, grid,
            vec["bo"], vec["s1"], vec["g2"], vec["b2"]]
    alias = {}
    if bufs is not None:
        alias = {1 + len(args) + j: j for j in range(len(bufs))}
        args = args + list(bufs)
        in_specs = in_specs + [pl.BlockSpec(memory_space=pl.ANY)] * len(bufs)
    return pl.pallas_call(
        functools.partial(skipping, attn_fwd_body),
        out_shape=shapes,
        grid_spec=pltpu.PrefetchScalarGridSpec(
            num_scalar_prefetch=1,
            grid=(groups,),
            in_specs=in_specs,
            out_specs=out_specs,
            scratch_shapes=[pltpu.VMEM((SPAN, d), BF16), pltpu.VMEM((SPAN, d), F32)],
        ),
        compiler_params=params(),
        input_output_aliases=alias,
        name="attn_fwd",
        cost_estimate=cost(22),
    )(sc, *args)


def mlp_fwd_body(sc, x, att, b, w1, c1, w2, c2, s1, s2, *rest):
    gs, ts, ms, ys, sent = rest[-6:-1]
    acc = rest[-1]
    step = pl.program_id(0)

    @pl.when(step == 0)
    def _():
        acc[...] = jnp.zeros_like(acc)

    h = dot_nn(b[0], w1[...]) + c1[...]
    cdf = 0.5 * (1.0 + lax.erf(h * (1.0 / math.sqrt(2.0))))
    g = (h * cdf).astype(BF16)
    slope = cdf + h * jnp.exp(-0.5 * h * h) * (1.0 / math.sqrt(2.0 * math.pi))
    gs[0] = g
    ts[0] = slope.astype(BF16)
    acc[...] += dot_nn(g, w2[...])

    @pl.when(step == pl.num_programs(0) - 1)
    def _():
        m = acc[...] + c2[...]
        ms[0] = m
        x1 = x[0].astype(F32) + s1[...] * att[0]
        y = ((x1 + s2[...] * m) * row_valid(sc)).astype(BF16)
        ys[0] = y
        sent[...] = y


FF_CHUNK = 1024


def mlp_fwd(sc, saved, vec, w1, w2, bufs):
    d, ff = w1.shape
    n = PIECES + 1
    xs, atts, bs = saved
    whole = pl.BlockSpec((1, d), lambda i, s: (0, 0))
    slot = lambda i, s: (s[0], 0, 0)
    chunk = lambda i, s: (s[0], 0, i * s[11])
    args = [xs, atts, bs, w1, vec["c1"], w2, vec["c2"], vec["s1"], vec["s2"]]
    in_specs = [
        pl.BlockSpec((1, SPAN, d), slot),
        pl.BlockSpec((1, SPAN, d), slot),
        pl.BlockSpec((1, SPAN, d), slot),
        pl.BlockSpec((d, FF_CHUNK), lambda i, s: (0, i * s[11])),
        pl.BlockSpec((1, FF_CHUNK), lambda i, s: (0, i * s[11])),
        pl.BlockSpec((FF_CHUNK, d), lambda i, s: (i * s[11], 0)),
        whole,
        whole,
        whole,
    ]
    alias = {}
    if bufs is not None:
        alias = {1 + len(args) + j: j for j in range(len(bufs))}
        args = args + list(bufs)
        in_specs = in_specs + [pl.BlockSpec(memory_space=pl.ANY)] * len(bufs)
    outs = pl.pallas_call(
        functools.partial(skipping, mlp_fwd_body),
        out_shape=[
            jax.ShapeDtypeStruct((n, SPAN, ff), BF16),
            jax.ShapeDtypeStruct((n, SPAN, ff), BF16),
            jax.ShapeDtypeStruct((n, SPAN, d), F32),
            jax.ShapeDtypeStruct((n, SPAN, d), BF16),
            jax.ShapeDtypeStruct((SPAN, d), BF16),
        ],
        grid_spec=pltpu.PrefetchScalarGridSpec(
            num_scalar_prefetch=1,
            grid=(ff // FF_CHUNK,),
            in_specs=in_specs,
            out_specs=[
                pl.BlockSpec((1, SPAN, FF_CHUNK), chunk),
                pl.BlockSpec((1, SPAN, FF_CHUNK), chunk),
                pl.BlockSpec((1, SPAN, d), slot),
                pl.BlockSpec((1, SPAN, d), slot),
                pl.BlockSpec((SPAN, d), lambda i, s: (0, 0)),
            ],
            scratch_shapes=[pltpu.VMEM((SPAN, d), F32)],
        ),
        compiler_params=params(),
        input_output_aliases=alias,
        name="mlp_fwd",
        cost_estimate=cost(16),
    )(sc, *args)
    return outs[:4], outs[4]


def incoming_rows(sc, cot, arr):
    dy = jnp.where(sc[2] == 0, arr[...], cot[0]).astype(F32)
    return dy * row_valid(sc)


def mlp_bwd_body(sc, cot, arr, x, att, m, slope, w1, w2, wo, s1, s2, g2, *rest):
    dms, dhs, d1s, das, dos, vecs, hbs = rest[-9:-2]
    dm_s, acc = rest[-2:]
    step = pl.program_id(0)

    @pl.when(step == 0)
    def _():
        dyv = incoming_rows(sc, cot, arr)
        d1s[0] = dyv
        dm = (s2[...] * dyv).astype(BF16)
        dm_s[...] = dm
        dms[0] = dm
        acc[...] = jnp.zeros_like(acc)
        vecs[0, 4:5] = col_sum(dm.astype(F32))
        vecs[0, 5:6] = col_sum(dyv * m[0])
        vecs[0, 6:8] = jnp.zeros_like(vecs[0, 6:8])

    dh = (dot_nt(dm_s[...], w2[...]) * slope[0].astype(F32)).astype(BF16)
    dhs[0] = dh
    hbs[0] = jnp.broadcast_to(col_sum(dh.astype(F32)), hbs.shape[1:])
    acc[...] += dot_nt(dh, w1[...])

    @pl.when(step == pl.num_programs(0) - 1)
    def _():
        x1 = x[0].astype(F32) + s1[...] * att[0]
        standard, inverse = standardise(x1)
        db = acc[...]
        dx1 = d1s[0] + norm_back(db, standard, inverse, g2[...])
        d1s[0] = dx1
        da = (s1[...] * dx1).astype(BF16)
        das[0] = da
        vecs[0, 0:1] = col_sum(da.astype(F32))
        vecs[0, 1:2] = col_sum(dx1 * att[0])
        vecs[0, 2:3] = col_sum(db * standard)
        vecs[0, 3:4] = col_sum(db)
        dos[0] = dot_nt(da, wo[...]).astype(BF16)


def mlp_bwd(sc, cot, arr, saved, vec, w1, w2, wo, bufs):
    d, ff = w1.shape
    n = PIECES + 1
    xs, atts, ms, ts = saved
    whole = pl.BlockSpec((1, d), lambda i, s: (0, 0))
    slot = lambda i, s: (s[0], 0, 0)
    read = lambda i, s: (s[1], 0, 0)
    chunk = lambda i, s: (s[0], 0, i * s[11])
    args = [cot, arr, xs, atts, ms, ts, w1, w2, wo, vec["s1"], vec["s2"], vec["g2"]]
    in_specs = [
        pl.BlockSpec((1, SPAN, d), read),
        pl.BlockSpec((SPAN, d), lambda i, s: (0, 0)),
        pl.BlockSpec((1, SPAN, d), read),
        pl.BlockSpec((1, SPAN, d), read),
        pl.BlockSpec((1, SPAN, d), read),
        pl.BlockSpec((1, SPAN, FF_CHUNK), lambda i, s: (s[1], 0, i * s[11])),
        pl.BlockSpec((d, FF_CHUNK), lambda i, s: (0, i * s[11])),
        pl.BlockSpec((FF_CHUNK, d), lambda i, s: (i * s[11], 0)),
        pl.BlockSpec((d, d), lambda i, s: (0, 0)),
        whole,
        whole,
        whole,
    ]
    alias = {}
    if bufs is not None:
        alias = {1 + len(args) + j: j for j in range(len(bufs))}
        args = args + list(bufs)
        in_specs = in_specs + [pl.BlockSpec(memory_space=pl.ANY)] * len(bufs)
    return pl.pallas_call(
        functools.partial(skipping, mlp_bwd_body),
        out_shape=[
            jax.ShapeDtypeStruct((n, SPAN, d), BF16),
            jax.ShapeDtypeStruct((n, SPAN, ff), BF16),
            jax.ShapeDtypeStruct((n, SPAN, d), F32),
            jax.ShapeDtypeStruct((n, SPAN, d), BF16),
            jax.ShapeDtypeStruct((n, SPAN, d), BF16),
            jax.ShapeDtypeStruct((n, 8, d), F32),
            jax.ShapeDtypeStruct((n, 8, ff), F32),
        ],
        grid_spec=pltpu.PrefetchScalarGridSpec(
            num_scalar_prefetch=1,
            grid=(ff // FF_CHUNK,),
            in_specs=in_specs,
            out_specs=[
                pl.BlockSpec((1, SPAN, d), slot),
                pl.BlockSpec((1, SPAN, FF_CHUNK), chunk),
                pl.BlockSpec((1, SPAN, d), slot),
                pl.BlockSpec((1, SPAN, d), slot),
                pl.BlockSpec((1, SPAN, d), slot),
                pl.BlockSpec((1, 8, d), slot),
                pl.BlockSpec((1, 8, FF_CHUNK), chunk),
            ],
            scratch_shapes=[pltpu.VMEM((SPAN, d), BF16), pltpu.VMEM((SPAN, d), F32)],
        ),
        compiler_params=params(),
        input_output_aliases=alias,
        name="mlp_bwd",
        cost_estimate=cost(19),
    )(sc, *args)


def attn_bwd_body(first, sc, x, d1, q, k, v, do, pg, plc, wq, wk, wv, g1, b1, *rest):
    dqs, dks, dvs, dxs, as_, vecs, bvs, dgs, sent = rest[-10:-1]
    acc = rest[-1]
    old = None if first else rest[0]
    step = pl.program_id(0)

    @pl.when(step == 0)
    def _():
        acc[...] = jnp.zeros_like(acc)

    zero = jnp.zeros((SPAN, 128), BF16)
    for pair in range(2):
        lanes = slice(pair * 128, pair * 128 + 128)
        qp, kp, vp, dp_ = q[0, :, lanes], k[0, :, lanes], v[0, :, lanes], do[0, :, lanes]
        total = [None] * (3 * len(BLOCKS))
        for hh in range(2):
            head = pair * 2 + hh
            mask = half_mask((SPAN, 128), hh)
            qm = jnp.where(mask, qp, zero)
            km = jnp.where(mask, kp, zero)
            vm = jnp.where(mask, vp, zero)
            dm = jnp.where(mask, dp_, zero)
            parts = []
            wide = local = None
            for glob, j, begin, size in BLOCKS:
                rows = slice(begin, begin + size)
                p = pg[0, head, j] if glob else plc[0, head, j]
                pb = p.astype(BF16)
                dp = dot_nt(dp_[rows], vm[rows])
                ds = (p * (dp - jnp.sum(dp * p, axis=-1, keepdims=True))).astype(BF16)
                if glob:
                    wide = ds.astype(F32) if wide is None else wide + ds.astype(F32)
                else:
                    local = ds.astype(F32) if local is None else local + ds.astype(F32)
                parts += [dot_nn(ds, km[rows]), dot_tn(ds, qm[rows]), dot_tn(pb, dm[rows])]
            dgs[0, head] = wide if first else jnp.where(sc[4] == 1, wide, old[0, head] + wide)
            dgs[0, head, :LPAD, :LPAD] += local
            total = [b if a is None else a + b for a, b in zip(total, parts)]
        for n, (_, _, begin, size) in enumerate(BLOCKS):
            rows = slice(begin, begin + size)
            dqs[0, rows, lanes] = total[3 * n].astype(BF16) * HEAD_DIM ** (-0.5)
            dks[0, rows, lanes] = total[3 * n + 1].astype(BF16)
            dvs[0, rows, lanes] = total[3 * n + 2].astype(BF16)
    dq, dk, dv = dqs[0], dks[0], dvs[0]
    bvs[0, 0:1] = col_sum(dq.astype(F32))
    bvs[0, 1:2] = col_sum(dv.astype(F32))
    bvs[0, 2:8] = jnp.zeros_like(bvs[0, 2:8])
    acc[...] += dot_nt(dq, wq[...]) + dot_nt(dk, wk[...]) + dot_nt(dv, wv[...])

    @pl.when(step == pl.num_programs(0) - 1)
    def _():
        standard, inverse = standardise(x[0].astype(F32))
        as_[0] = (standard * g1[...] + b1[...]).astype(BF16)
        da = acc[...]
        dx = (d1[0] + norm_back(da, standard, inverse, g1[...])).astype(BF16)
        dxs[0] = dx
        sent[...] = dx
        vecs[0, 0:1] = col_sum(da * standard)
        vecs[0, 1:2] = col_sum(da)
        vecs[0, 2:8] = jnp.zeros_like(vecs[0, 2:8])


def attn_bwd(sc, saved, vec, wa, bufs, dgrid):
    xs, d1s, qs, ks, vs, dos, pgs, pls = saved
    d = xs.shape[-1]
    heads = pgs.shape[1]
    groups = d // 256
    per = heads // groups
    n = PIECES + 1
    whole = pl.BlockSpec((1, d), lambda i, s: (0, 0))
    slot = lambda i, s: (s[0], 0, 0)
    read = lambda i, s: (s[1], 0, 0)
    now = lambda i, s: (s[0], 0, 0)
    chunk = lambda i, s: (s[0], 0, i * s[11])
    first = dgrid is None
    rchunk = pl.BlockSpec((1, SPAN, 256), lambda i, s: (s[1], 0, i * s[11]))
    grid_spec = pl.BlockSpec((1, per, GPAD, GPAD), lambda i, s: (s[3], i * s[11], 0, 0))
    args = [xs, d1s, qs, ks, vs, dos, pgs, pls, wa, wa, wa, vec["g1"], vec["b1"]]
    in_specs = [
        pl.BlockSpec((1, SPAN, d), read),
        pl.BlockSpec((1, SPAN, d), now),
        rchunk,
        rchunk,
        rchunk,
        pl.BlockSpec((1, SPAN, 256), chunk),
        pl.BlockSpec((1, per, 2, GPAD, GPAD), lambda i, s: (s[1], i * s[11], 0, 0, 0)),
        pl.BlockSpec((1, per, 4, LPAD, LPAD), lambda i, s: (s[1], i * s[11], 0, 0, 0)),
        pl.BlockSpec((d, 256), lambda i, s: (0, i * s[11])),
        pl.BlockSpec((d, 256), lambda i, s: (0, groups + i * s[11])),
        pl.BlockSpec((d, 256), lambda i, s: (0, 2 * groups + i * s[11])),
        whole,
        whole,
    ]
    alias = {}
    if not first:
        alias[1 + len(args)] = 7
        args = args + [dgrid]
        in_specs = in_specs + [grid_spec]
        for j in range(len(bufs)):
            alias[1 + len(args) + j] = j
        args = args + list(bufs)
        in_specs = in_specs + [pl.BlockSpec(memory_space=pl.ANY)] * len(bufs)
    outs = pl.pallas_call(
        functools.partial(skipping, functools.partial(attn_bwd_body, first)),
        out_shape=[
            jax.ShapeDtypeStruct((n, SPAN, d), BF16),
            jax.ShapeDtypeStruct((n, SPAN, d), BF16),
            jax.ShapeDtypeStruct((n, SPAN, d), BF16),
            jax.ShapeDtypeStruct((n, SPAN, d), BF16),
            jax.ShapeDtypeStruct((n, SPAN, d), BF16),
            jax.ShapeDtypeStruct((n, 8, d), F32),
            jax.ShapeDtypeStruct((n, 8, d), F32),
            jax.ShapeDtypeStruct((2, heads, GPAD, GPAD), F32),
            jax.ShapeDtypeStruct((SPAN, d), BF16),
        ],
        grid_spec=pltpu.PrefetchScalarGridSpec(
            num_scalar_prefetch=1,
            grid=(groups,),
            in_specs=in_specs,
            out_specs=[
                pl.BlockSpec((1, SPAN, 256), chunk),
                pl.BlockSpec((1, SPAN, 256), chunk),
                pl.BlockSpec((1, SPAN, 256), chunk),
                pl.BlockSpec((1, SPAN, d), slot),
                pl.BlockSpec((1, SPAN, d), slot),
                pl.BlockSpec((1, 8, d), slot),
                pl.BlockSpec((1, 8, 256), chunk),
                grid_spec,
                pl.BlockSpec((SPAN, d), lambda i, s: (0, 0)),
            ],
            scratch_shapes=[pltpu.VMEM((SPAN, d), F32)],
        ),
        compiler_params=params(),
        input_output_aliases=alias,
        name="attn_bwd",
        cost_estimate=cost(26),
    )(sc, *args)
    return outs[:7], outs[7], outs[8]


def weight_body(pairs, last, sc, *refs):
    lefts, rights = refs[:pairs], refs[pairs : 2 * pairs]
    refs = refs[2 * pairs :]
    if last:
        arr, scale = refs[:2]
        refs = refs[2:]
    keep, send = refs[:2]
    step = pl.program_id(0)
    half = pl.num_programs(0) // 2
    rows = PIECES * SPAN
    if last:
        dm_s = refs[2]

        @pl.when(step == 0)
        def _():
            for p in range(PIECES - 1):
                dm_s[p * SPAN : (p + 1) * SPAN] = rights[0][p]
            dy = arr[...].astype(F32) * row_valid(sc)
            fresh = (scale[...] * dy).astype(BF16)
            dm_s[rows - SPAN : rows] = jnp.where(sc[2] == 0, fresh, rights[0][PIECES - 1])

    parts = []
    for left, right in zip(lefts, rights):
        a = left[...].reshape(rows, left.shape[2])
        b = dm_s[...] if last else right[...].reshape(rows, right.shape[2])
        parts.append(dot_tn(a, b).astype(BF16))

    @pl.when(step < half)
    def _():
        for j, part in enumerate(parts):
            send[:, j * part.shape[1] : (j + 1) * part.shape[1]] = part

    @pl.when(step >= half)
    def _():
        for j, part in enumerate(parts):
            keep[:, j * part.shape[1] : (j + 1) * part.shape[1]] = part


def weight_grad(sc, pairs, rows, block, us, last=None, columns=None):
    offset, count = rows
    half = count // 2 // block
    assert half * 2 * block == count and offset % block == 0
    first = offset // block

    def source(i, s):
        other = jnp.where(i < half, 1 - s[12], s[12])
        return first + other * half + jnp.where(i < half, i, i - half)

    begin, wide = columns or (0, pairs[0][1].shape[2])
    assert begin % wide == 0
    width = wide * len(pairs)
    in_specs = [
        pl.BlockSpec((PIECES, SPAN, block), lambda i, s: (0, 0, source(i, s))) for _ in pairs
    ] + [
        pl.BlockSpec((PIECES, SPAN, wide), lambda i, s: (0, 0, begin // wide)) for _ in pairs
    ]
    args = [left for left, _ in pairs] + [right for _, right in pairs]
    scratch = []
    if last is not None:
        d = last[0].shape[1]
        in_specs += [
            pl.BlockSpec((SPAN, d), lambda i, s: (0, 0)),
            pl.BlockSpec((1, d), lambda i, s: (0, 0)),
        ]
        args += list(last)
        scratch = [pltpu.VMEM((PIECES * SPAN, d), BF16)]
    return pl.pallas_call(
        functools.partial(weight_body, len(pairs), last is not None),
        out_shape=[jax.ShapeDtypeStruct((count // 2, width), BF16)] * 2,
        grid_spec=pltpu.PrefetchScalarGridSpec(
            num_scalar_prefetch=1,
            grid=(2 * half,),
            in_specs=in_specs,
            out_specs=[
                pl.BlockSpec((block, width), lambda i, s: (jnp.maximum(i - half, 0), 0)),
                pl.BlockSpec((block, width), lambda i, s: (jnp.minimum(i, half - 1), 0)),
            ],
            scratch_shapes=scratch,
        ),
        compiler_params=params(),
        cost_estimate=cost(us),
        name="weight_grad",
    )(sc, *args)


TABLE = 768
INNER = 256
OUTER = TABLE // INNER
ROWS = 16


def one_hot(index_row):
    outer = lax.shift_right_logical(index_row, 8)
    inner = index_row - outer * INNER
    high = lax.shift_right_logical(inner, 4)
    low = inner - high * 16
    rows = lax.broadcasted_iota(jnp.int32, (16, GPAD), 0)
    block = jnp.where(rows == low, 1.0, 0.0).astype(BF16)
    which = jnp.broadcast_to(high.astype(F32), (16, GPAD)).astype(BF16)
    zero = jnp.zeros((16, GPAD), BF16)
    hot = [jnp.where(which == jnp.bfloat16(a), block, zero) for a in range(INNER // 16)]
    return jnp.concatenate(hot, axis=0), outer


def grid_body(table, index, out):
    heads = out.shape[0]
    column = lax.broadcasted_iota(jnp.int32, (16, GPAD), 1)
    for r in range(ROWS):
        hot, outer = one_hot(index[r : r + 1, :])
        parts = dot_nn(table[...], hot)
        values = jnp.zeros((16, GPAD), F32)
        for a in range(OUTER):
            own = parts[a * 32 : a * 32 + 16] + parts[a * 32 + 16 : a * 32 + 32]
            values = jnp.where(outer == a, own, values)
        values = jnp.where(column < GLOB, values, NEGATIVE)
        for h in range(heads):
            out[h, r : r + 1, :] = values[h : h + 1]


def build_grid(table, index):
    rows, heads = table.shape
    flat = jnp.pad(table.T, ((0, 16 - heads), (0, TABLE - rows)))
    high = flat.astype(BF16)
    low = (flat - high.astype(F32)).astype(BF16)
    stacked = jnp.concatenate(
        [part[:, a * INNER : (a + 1) * INNER] for a in range(OUTER) for part in (high, low)], axis=0
    )
    return pl.pallas_call(
        grid_body,
        out_shape=jax.ShapeDtypeStruct((heads, GPAD, GPAD), F32),
        grid=(GPAD // ROWS,),
        in_specs=[
            pl.BlockSpec((32 * OUTER, INNER), lambda i: (0, 0)),
            pl.BlockSpec((ROWS, GPAD), lambda i: (i, 0)),
        ],
        out_specs=pl.BlockSpec((heads, ROWS, GPAD), lambda i: (0, i, 0)),
        compiler_params=params(),
        name="build_grid",
        cost_estimate=cost(8),
    )(stacked, index)


def table_body(sc, index, dg, out):
    step = pl.program_id(0)
    heads = dg.shape[1]

    @pl.when(step == 0)
    def _():
        out[...] = jnp.zeros_like(out)

    total = jnp.zeros((32 * OUTER, INNER), F32)
    pad = jnp.zeros((16 - heads, GPAD), F32)
    for r in range(ROWS):
        hot, outer = one_hot(index[r : r + 1, :])
        rows = jnp.concatenate([dg[0, h, r : r + 1, :] for h in range(heads)] + [pad], axis=0)
        high = rows.astype(BF16).astype(F32)
        both = jnp.concatenate([high, rows - high], axis=0)
        left = jnp.concatenate([jnp.where(outer == a, both, 0.0) for a in range(OUTER)], axis=0)
        total += dot_nt(left.astype(BF16), hot)
    out[...] += total


def table_grad(sc, index, dgrid):
    heads = dgrid.shape[1]
    out = pl.pallas_call(
        table_body,
        out_shape=jax.ShapeDtypeStruct((32 * OUTER, INNER), F32),
        grid_spec=pltpu.PrefetchScalarGridSpec(
            num_scalar_prefetch=1,
            grid=(GPAD // ROWS,),
            in_specs=[
                pl.BlockSpec((ROWS, GPAD), lambda i, s: (i, 0)),
                pl.BlockSpec((1, heads, ROWS, GPAD), lambda i, s: (0, 0, i, 0)),
            ],
            out_specs=pl.BlockSpec((32 * OUTER, INNER), lambda i, s: (0, 0)),
        ),
        compiler_params=params(),
        name="table_grad",
        cost_estimate=cost(18),
    )(sc, index, dgrid)
    parts = [out[a * 32 : a * 32 + 16] + out[a * 32 + 16 : a * 32 + 32] for a in range(OUTER)]
    return jnp.concatenate(parts, axis=1)


def unpack_body(pieces, out):
    own = pieces[0].astype(F32)
    parts = [own[begin : begin + GLOB] for glob, _, begin, _ in BLOCKS if glob]
    parts += [own[begin : begin + LOC] for glob, _, begin, _ in BLOCKS if not glob]
    tail = out.shape[1] - 2 * GLOB - 4 * LOC
    parts.append(jnp.zeros((tail, own.shape[1]), F32))
    out[0] = jnp.concatenate(parts, axis=0).astype(BF16)


def unpack(pieces, slot_rows):
    d = pieces.shape[2]
    return pl.pallas_call(
        unpack_body,
        out_shape=jax.ShapeDtypeStruct((PIECES, slot_rows, d), BF16),
        grid=(PIECES,),
        in_specs=[pl.BlockSpec((1, SPAN, d), lambda i: (i, 0, 0))],
        out_specs=pl.BlockSpec((1, slot_rows, d), lambda i: (i, 0, 0)),
        compiler_params=params(),
        cost_estimate=cost(3),
        name="unpack",
    )(pieces)


def pack(rows):
    pieces = []
    for m in range(rows.shape[0]):
        parts = []
        for glob, j, _, size in BLOCKS:
            length = GLOB if glob else LOC
            begin = j * GLOB if glob else 2 * GLOB + j * LOC
            parts.append(jnp.pad(rows[m, begin : begin + length], ((0, size - length), (0, 0))))
        pieces.append(jnp.concatenate(parts, axis=0))
    return jnp.stack(pieces)


def exchange(value, bit):
    peers = lax.axis_size("dp")
    return lax.ppermute(value, "dp", [(i, i ^ (1 << bit)) for i in range(peers)])


def own_bit(bit):
    return (lax.axis_index("dp") >> bit) & 1


class Small:
    def __init__(self, value, order):
        self.value = value
        self.left = list(order)
        self.done = False

    def begin(self):
        return exchange(self.value, self.left[0])

    def finish(self, got):
        self.value = self.value + got
        self.left = self.left[1:]
        self.done = not self.left


class Job:
    def __init__(self, parts, order):
        self.keep, self.send = parts
        self.order = order
        self.place = 0
        self.back = False
        self.done = False

    def begin(self):
        bit = self.order[self.place]
        return exchange(self.keep if self.back else self.send, bit)

    def finish(self, got):
        bit = self.order[self.place]
        if self.back:
            part = self.keep
            self.keep = jnp.where(
                own_bit(bit) == 0,
                jnp.concatenate([part, got], axis=0),
                jnp.concatenate([got, part], axis=0),
            )
            self.place -= 1
            self.done = self.place < 0
            return
        if self.place + 1 == len(self.order):
            self.keep = (self.keep.astype(F32) + got.astype(F32)).astype(BF16)
            self.back = True
            return
        half = self.keep.shape[0] // 2
        following = own_bit(self.order[self.place + 1])
        keep = self.keep

        def part(side):
            a = lax.dynamic_slice_in_dim(keep, side * half, half, 0)
            b = lax.dynamic_slice_in_dim(got, side * half, half, 0)
            return (a.astype(F32) + b.astype(F32)).astype(BF16)

        self.keep, self.send = part(following), part(1 - following)
        self.place += 1


def advance(gate, jobs):
    gate, *got = lax.optimization_barrier((gate, *[job.begin() for job in jobs]))
    for job, value in zip(jobs, got):
        job.finish(value)
    return gate


def body(
    tokens,
    cotangent,
    crop_lengths,
    relative_index,
    first_gain,
    first_shift,
    attend_weight,
    query_bias,
    value_bias,
    relative_table,
    output_weight,
    output_bias,
    scale_one,
    second_gain,
    second_shift,
    expand_weight,
    expand_bias,
    reduce_weight,
    reduce_bias,
    scale_two,
):
    micro, slot_rows, d = tokens.shape
    assert micro == PIECES and crop_lengths.shape[1] == 1
    pipe = lax.axis_index("pipe")
    vec = dict(
        g1=first_gain, b1=first_shift, bq=query_bias, bv=value_bias, bo=output_bias,
        s1=scale_one, g2=second_gain, b2=second_shift, c1=expand_bias, c2=reduce_bias, s2=scale_two,
    )
    wa, wo, w1, w2 = attend_weight[0], output_weight[0], expand_weight[0], reduce_weight[0]
    table = relative_table[0]
    index = jnp.pad(relative_index, ((0, GPAD - GLOB), (0, GPAD - GLOB)))
    tok, cot = pack(tokens), pack(cotangent)
    grid = build_grid(table, index)
    blank = jnp.zeros((SPAN, d), BF16)
    own = crop_lengths[:, 0, :]
    lengths = jnp.concatenate([own[:, :1], own[:, 2:4], own[:, 1:2], own[:, 4:6]], axis=1)

    def scalars(section):
        piece = jnp.arange(PIECES, dtype=jnp.int32)
        ones = jnp.ones_like(piece)
        active = ones * (pipe == section)
        columns = [
            jnp.where(active == 1, piece, PIECES), piece, ones * pipe, 1 - active,
            jnp.where(piece == 0, 1, 0),
        ]
        crops = [lengths[:, j] for j in range(lengths.shape[1])]
        columns += crops + [active, ones * own_bit(0)]
        return jnp.stack(columns, axis=1).astype(jnp.int32)

    calls = [scalars(0), scalars(1)]
    attn = mlp = None
    moving = [blank] * PIECES
    for section in range(2):
        for p in range(PIECES):
            sc = calls[section][p]
            attn = attn_fwd(sc, tok, moving[p], vec, wa, wo, grid, attn)
            mlp, sent = mlp_fwd(sc, (attn[0], attn[7], attn[8]), vec, w1, w2, mlp)
            if section == 0:
                moving[p] = lax.ppermute(sent, "pipe", [(0, 1)])
    xs, qs, ks, vs, pgs, pls, os_, atts, bs = attn
    gs, ts, ms, ys = mlp
    ff = w1.shape[1]
    first = second = dgrid = None
    moving = [blank] * PIECES
    bits = lax.axis_size("dp").bit_length() - 1
    plain = list(range(bits))
    other = [plain[0], plain[2], plain[1]] + plain[3:]
    for section in (1, 0):
        for p in range(PIECES):
            sc = calls[section][p]
            arr = moving[p]
            final = section == 0 and p == PIECES - 1
            if final:
                second = list(second)
                sc, second[5] = lax.optimization_barrier((sc, second[5]))
                a, b = [
                    Job(
                        weight_grad(
                            sc, [(gs, first[0])], (r * ff // 2, ff // 2), 384, 8, (arr, vec["s2"])
                        ),
                        plain,
                    )
                    for r in range(2)
                ]
                sc, b.keep, b.send = lax.optimization_barrier((sc, b.keep, b.send))
                sc = advance(sc, [a])
            first = mlp_bwd(sc, cot, arr, (xs, atts, ms, ts), vec, w1, w2, wo, first)
            if final:
                sc = advance(sc, [a, b])
                c, e = [
                    Job(
                        weight_grad(
                            sc, [(bs, first[1])], (0, d), 128, 9, columns=(r * ff // 2, ff // 2)
                        ),
                        order,
                    )
                    for r, order in enumerate((plain, other))
                ]
                sc = advance(sc, [a, b])
                sc = advance(sc, [c])
            second, dgrid, sent = attn_bwd(
                sc, (xs, first[2], qs, ks, vs, first[4], pgs, pls), vec, wa, second, dgrid
            )
            if section == 1:
                moving[p] = lax.ppermute(sent, "pipe", [(1, 0)])
    dms, dhs, d1s, das, dos, late, late_bias = first
    dqs, dks, dvs, dxs, as_, early, early_bias = second

    sc = advance(sc, [a, b, c, e])
    q = Job(weight_grad(sc, [(os_, das), (as_, dqs)], (0, d), 384, 9), plain)
    k = Job(weight_grad(sc, [(as_, dks), (as_, dvs)], (0, d), 384, 9), plain)
    sc = advance(sc, [a, b, c, e])
    d_table = table_grad(sc, index, dgrid)
    small = jnp.concatenate(
        [
            jnp.sum(late[:PIECES, :6], axis=0).reshape(-1),
            jnp.sum(early[:PIECES, :2], axis=0).reshape(-1),
            jnp.sum(early_bias[:PIECES, :2], axis=0).reshape(-1),
            jnp.sum(late_bias[:PIECES, 0], axis=0),
            d_table.reshape(-1),
        ]
    ).reshape(-1, d)
    s = Small(small, plain)
    tail = [[a, b, c, e, q, k], [q, c, e, b], [k, q, c, e], [a, k, q, s], [b, k, q, a, s]]
    tail += [[c, e, k, q, b, s], [q, k, c, s], [k, e, q], [k, e]]
    for jobs in tail:
        sc = advance(sc, [job for job in jobs if not job.done])
    everything = [a, b, c, e, q, k, s]
    while not all(job.done for job in everything):
        sc = advance(sc, [job for job in everything if not job.done])
    small = s.value
    whole = [job.keep.astype(F32) for job in (a, b, c, e, q, k)]
    reduce_grad = jnp.concatenate(whole[:2], axis=0)
    expand_grad = jnp.concatenate(whole[2:4], axis=1)
    output_grad = whole[4][:, :d]
    attend_grad = jnp.concatenate([whole[4][:, d:], whole[5]], axis=1)
    expand_bias_grad = small[10 : 10 + ff // d].reshape(-1)
    table_sum = small[10 + ff // d :].reshape(16, -1)[: table.shape[1], : table.shape[0]].T
    ordered = (
        small[6], small[7], attend_grad, small[8], small[9], table_sum, output_grad,
        small[0], small[1], small[2], small[3], expand_grad, expand_bias_grad, reduce_grad,
        small[4], small[5],
    )
    outputs = unpack(ys, slot_rows)
    grads = unpack(dxs, slot_rows)
    return (outputs[None], grads[None]) + tuple(member[None] for member in ordered)


def solution(mesh):
    in_specs = (
        P(None, "dp", None),
        P(None, "dp", None),
        P(None, "dp", None),
        P(),
        P("pipe", None),
        P("pipe", None),
        P("pipe", None, None),
        P("pipe", None),
        P("pipe", None),
        P("pipe", None, None),
        P("pipe", None, None),
        P("pipe", None),
        P("pipe", None),
        P("pipe", None),
        P("pipe", None),
        P("pipe", None, None),
        P("pipe", None),
        P("pipe", None, None),
        P("pipe", None),
        P("pipe", None),
    )
    out_specs = (
        P("pipe", None, "dp", None),
        P("pipe", None, "dp", None),
        P("pipe", None),
        P("pipe", None),
        P("pipe", None, None),
        P("pipe", None),
        P("pipe", None),
        P("pipe", None, None),
        P("pipe", None, None),
        P("pipe", None),
        P("pipe", None),
        P("pipe", None),
        P("pipe", None),
        P("pipe", None, None),
        P("pipe", None),
        P("pipe", None, None),
        P("pipe", None),
        P("pipe", None),
    )
    return jax.shard_map(body, mesh=mesh, in_specs=in_specs, out_specs=out_specs, check_vma=False)
```
